768 devices in a mesh: curve: 96 (over x, z, core), tile: 8 (over y).
Axes of the slice: x: 4, y: 8, z: 12, core: 2. Of those that a mesh axis runs over, the one named last changes fastest.
Arguments:
- state: float32 [5, 24576, 512], P(None, ('curve', 'tile')), may hold values from -6 to 6
- levels: int32 [24576], P(('curve', 'tile')), may hold values from 0 to 2
- send_faces: int32 [6144, 2], P(('curve', 'tile')), may hold values from 0 to 959, as said below
- send_counts: int32 [6144], P(('curve', 'tile')), may hold values from 0 to 2, as said below
- recv_faces: int32 [6144, 2], P(('curve', 'tile')), may hold values from 0 to 191, as said below
- recv_orients: int32 [6144, 2], P(('curve', 'tile')), may hold values from 0 to 7, as said below
- recv_counts: int32 [6144], P(('curve', 'tile')), may hold values from 0 to 2
- curve_faces: int32 [1536, 16], P(('curve', 'tile')), may hold values from 0 to 191, as said below
- curve_orients: int32 [1536, 16], P(('curve', 'tile')), may hold values from 0 to 7, as said below
- curve_counts: int32 [1536], P(('curve', 'tile')), may hold values from 0 to 16, as said below
Outputs:
- advanced: float32 [5, 24576, 512], P(None, ('curve', 'tile'))
The draws below stay inside these ranges and needn't reach their ends.
Inputs may be any that keep to these rules, and one draw needn't show every extreme that they name: `send_faces`: row p of device (b, t) lists in its first send_counts entries the pairs it shares with device (b, p): (6 e + f) 5 + c with f 3 or 5 and c 0 to 3 for a half-face mortar of a coarse face, 4 for a whole face; each coarse face listed has its four children 0 to 3 listed once each, possibly with different peers; any other face id appears at most once in all lists of a device; entries past the count are 0. `send_counts`: the count of device (b, t) for peer p equals the receive count of device (b, p) for peer t. `recv_faces`: slot k of row t of device (b, p) is face 6 e + f paired with slot k of row p of device (b, t), with f = 2 where the sender's face is 3 and 4 where it is 5; entries past the count are 0. `recv_orients`: R_o maps the sender's node order into the receiver's; 0 past the count. `curve_faces`: row 0 names faces with f = 0, row 1 faces with f = 1; slot k of row 1 of device (b, t) pairs with slot k of row 0 of device (b + 1, t); entries past the count are 0. `curve_orients`: the two sides of a pair hold mutually inverse orientations; 0 past the count. `curve_counts`: both sides of a pair of rows hold the same count; it is 0 towards a curve index that does not exist.
All inputs are finite; a program needn't handle non-finite values.
Results may differ from the reference program's by a relative error of at most 0.0003.
Values sent between devices are 32-bit elements; how exact they have to be, the bound alone decides.
No kernel may reach another device: no remote copies, remote signals or barrier semaphores. Data moves between devices by JAX's collectives and lax.ppermute only.
A program may use at most 64 MiB of HBM per device.

```python
import jax
import jax.numpy as jnp
import numpy as np
from jax import lax

FIELDS = 5
NODES = 512
E_DEV = 32
ELEMS = 24576
CAPM = 2
CAPH = 16
N_CURVE = 96
N_TILE = 8


def orient_inverse():
    perm_table = np.zeros((8, 64), np.int64)
    for orient_code in range(8):
        for first_at in range(8):
            for second_at in range(8):
                if orient_code & 4:
                    upper_at, lower_at = (second_at, first_at)
                else:
                    upper_at, lower_at = (first_at, second_at)
                if orient_code & 1:
                    upper_at = 7 - upper_at
                if orient_code & 2:
                    lower_at = 7 - lower_at
                perm_table[orient_code, 8 * first_at + second_at] = 8 * upper_at + lower_at
    inverse = np.zeros((8,), np.int32)
    for first_at in range(8):
        for second_at in range(8):
            if int(np.sum(perm_table[first_at][perm_table[second_at]] == np.arange(64))) == 64:
                inverse[first_at] = second_at
    return inverse


def shuffles(base_key, row_count, row_width):

    def one_row(row_key):
        return jax.random.permutation(row_key, row_width)
    return jax.vmap(one_row)(jax.random.split(base_key, row_count)).astype(jnp.int32)


def live_ranks(base_key, live_grid):
    row_count, row_width = live_grid.shape
    shuffled = shuffles(base_key, row_count, row_width)
    scores = jnp.where(live_grid, shuffled, shuffled + row_width)
    ranked = jnp.argsort(scores, axis=1, stable=True)
    return jnp.argsort(ranked, axis=1, stable=True).astype(jnp.int32)


def build_lists(base_key):
    subkeys = jax.random.split(jax.random.fold_in(base_key, 91357), 12)
    devices = N_CURVE * N_TILE
    unit_total = N_TILE * CAPM
    busy_tile = jax.random.randint(subkeys[0], (N_CURVE,), 0, N_TILE)
    light_load = jnp.minimum(jax.random.randint(subkeys[1], (N_CURVE, N_TILE, N_TILE), 0, max(2, CAPM // 2 + 1)), CAPM)
    peer_ids = jnp.arange(N_TILE)
    send_count = jnp.where(peer_ids[None, None, :] == busy_tile[:, None, None], CAPM, light_load).astype(jnp.int32)
    live_grid = jnp.arange(CAPM) < send_count[..., None]
    send_live = live_grid.reshape(devices, unit_total)
    send_rank = live_ranks(subkeys[2], send_live)
    live_total = jnp.sum(send_live.astype(jnp.int32), axis=1, keepdims=True)
    coarse_total = live_total // 5
    is_coarse = send_rank < 4 * coarse_total
    unit_ids = jnp.where(is_coarse, send_rank // 4, send_rank - 3 * coarse_total)
    child_ids = jnp.where(is_coarse, send_rank % 4, 4)
    send_elems = jnp.take_along_axis(shuffles(subkeys[3], devices, E_DEV), unit_ids, axis=1)
    unit_bits = jnp.take_along_axis(jax.random.randint(subkeys[4], (devices, unit_total), 0, 2), unit_ids, axis=1)
    send_face = jnp.where(send_live, (send_elems * 6 + 3 + 2 * unit_bits) * 5 + child_ids, 0)
    recv_live = jnp.transpose(live_grid, (0, 2, 1, 3)).reshape(devices, unit_total)
    recv_bits = jnp.transpose(unit_bits.reshape(N_CURVE, N_TILE, N_TILE, CAPM), (0, 2, 1, 3)).reshape(devices, unit_total)
    recv_rank = live_ranks(subkeys[5], recv_live)
    recv_elems = jnp.take_along_axis(shuffles(subkeys[6], devices, E_DEV), recv_rank, axis=1)
    recv_face = jnp.where(recv_live, recv_elems * 6 + 2 + 2 * recv_bits, 0)
    recv_orient = jnp.where(recv_live, jax.random.randint(subkeys[7], (devices, unit_total), 0, 8), 0)
    recv_count = jnp.transpose(send_count, (0, 2, 1))
    edge_count = jax.random.randint(subkeys[8], (N_CURVE - 1, N_TILE), CAPH - CAPH // 2, CAPH + 1)
    full_edge = jax.random.randint(subkeys[9], (N_TILE,), 0, N_CURVE - 1)
    edge_count = jnp.where(jnp.arange(N_CURVE - 1)[:, None] == full_edge[None, :], CAPH, edge_count).astype(jnp.int32)
    zero_row = jnp.zeros((1, N_TILE), jnp.int32)
    curve_count = jnp.stack([jnp.concatenate([zero_row, edge_count], 0), jnp.concatenate([edge_count, zero_row], 0)], axis=2)
    curve_live = jnp.arange(CAPH) < curve_count[..., None]
    edge_orient = jax.random.randint(subkeys[10], (N_CURVE - 1, N_TILE, CAPH), 0, 8)
    inverse = jnp.asarray(orient_inverse(), jnp.int32)
    inverse_edge = jnp.sum((edge_orient[..., None] == jnp.arange(8)).astype(jnp.int32) * inverse, axis=-1)
    zero_plane = jnp.zeros((1, N_TILE, CAPH), jnp.int32)
    curve_orient = jnp.stack([jnp.concatenate([zero_plane, inverse_edge], 0), jnp.concatenate([edge_orient, zero_plane], 0)], axis=2)
    curve_orient = jnp.where(curve_live, curve_orient, 0)
    curve_elems = shuffles(subkeys[11], devices, E_DEV)[:, :CAPH].reshape(N_CURVE, N_TILE, 1, CAPH)
    curve_face = jnp.where(curve_live, curve_elems * 6 + jnp.arange(2).reshape(1, 1, 2, 1), 0)
    return (send_face, send_count, recv_face, recv_orient, recv_count, curve_face, curve_orient, curve_count)


def draw_send_faces(key, part):
    return build_lists(key)[0].reshape(N_CURVE * N_TILE * N_TILE, CAPM).astype(jnp.int32)


def draw_send_counts(key, part):
    return build_lists(key)[1].reshape(-1).astype(jnp.int32)


def draw_recv_faces(key, part):
    return build_lists(key)[2].reshape(N_CURVE * N_TILE * N_TILE, CAPM).astype(jnp.int32)


def draw_recv_orients(key, part):
    return build_lists(key)[3].reshape(N_CURVE * N_TILE * N_TILE, CAPM).astype(jnp.int32)


def draw_recv_counts(key, part):
    return build_lists(key)[4].reshape(-1).astype(jnp.int32)


def draw_curve_faces(key, part):
    return build_lists(key)[5].reshape(N_CURVE * N_TILE * 2, CAPH).astype(jnp.int32)


def draw_curve_orients(key, part):
    return build_lists(key)[6].reshape(N_CURVE * N_TILE * 2, CAPH).astype(jnp.int32)


def draw_curve_counts(key, part):
    return build_lists(key)[7].reshape(-1).astype(jnp.int32)


def with_ends(drawn, stream_key, low, high):
    longest = drawn.shape.index(max(drawn.shape))
    spots = []
    for shift in (0, 1):
        where = [jax.random.randint(jax.random.fold_in(stream_key, axis), (), 0, length) for axis, length in enumerate(drawn.shape)]
        where[longest] = (where[longest] + shift) % drawn.shape[longest]
        spots.append(tuple(where))
    return drawn.at[spots[0]].set(low).at[spots[1]].set(high)


def block_levels(own_key, dims, cuts, smallest, largest):
    def one(axis_at, shards_of):
        heights = jax.random.uniform(jax.random.fold_in(jax.random.fold_in(own_key, 6), axis_at), (shards_of,), jnp.float32, smallest / len(cuts), largest / len(cuts))
        return jnp.repeat(jnp.exp(heights), dims[axis_at] // shards_of).reshape((-1,) + (1,) * (len(dims) - axis_at - 1))

    factor_of = one(*cuts[0])
    for cut in cuts[1:]:
        factor_of = factor_of * one(*cut)
    return factor_of


def normal_values(own_key, extent, scale, limit, cuts=(), kind=jnp.bfloat16):
    values = jax.random.normal(own_key, extent, jnp.float32) * scale
    if len(cuts) > 0:
        values = block_levels(own_key, extent, cuts, -0.22, 0.18) * values
    return jnp.clip(values, min=-limit, max=limit).astype(kind)


def setup_inputs(seed: int = 0) -> dict:
    seeds = jax.random.split(jax.random.key(seed), 11)
    return {
        "state": normal_values(seeds[0], (FIELDS, ELEMS, NODES), 1.0, 6.0, ((1, 768),), jnp.float32),
        "levels": with_ends(jax.random.randint(seeds[1], (ELEMS,), 0, 3), jax.random.fold_in(seeds[1], 1), 0, 2).astype(jnp.int32),
        "send_faces": draw_send_faces(jax.random.fold_in(seeds[10], 71), 0),
        "send_counts": draw_send_counts(jax.random.fold_in(seeds[10], 71), 0),
        "recv_faces": draw_recv_faces(jax.random.fold_in(seeds[10], 71), 0),
        "recv_orients": draw_recv_orients(jax.random.fold_in(seeds[10], 71), 0),
        "recv_counts": draw_recv_counts(jax.random.fold_in(seeds[10], 71), 0),
        "curve_faces": draw_curve_faces(jax.random.fold_in(seeds[10], 71), 0),
        "curve_orients": draw_curve_orients(jax.random.fold_in(seeds[10], 71), 0),
        "curve_counts": draw_curve_counts(jax.random.fold_in(seeds[10], 71), 0),
    }


time_step = 0.002
wave_speed = 1.0
highest = lax.Precision.HIGHEST
inner_nodes = [-0.8717401485096066153374457, -0.5917001814331423021445107, -0.2092992179024788687686573,
               0.2092992179024788687686573, 0.5917001814331423021445107, 0.8717401485096066153374457]


def legendre_seven(abscissa):
    before = abscissa * 0.0 + 1.0
    current = abscissa + 0.0
    for order in range(1, 7):
        before, current = current, ((2 * order + 1) * abscissa * current - order * before) / (order + 1)
    return current


def basis_tables():
    degree = 7
    points = np.array([-1.0] + inner_nodes + [1.0])
    values = legendre_seven(points)
    weights = 2.0 / (degree * (degree + 1) * values ** 2)
    deriv_mat = np.zeros((8, 8))
    for row_at in range(8):
        for col_at in range(8):
            if row_at != col_at:
                deriv_mat[row_at, col_at] = values[row_at] / (values[col_at] * (points[row_at] - points[col_at]))
    deriv_mat[0, 0] = -degree * (degree + 1) / 4.0
    deriv_mat[7, 7] = degree * (degree + 1) / 4.0
    halves = []
    projections = []
    for half_side in range(2):
        targets = (points + 2.0 * half_side - 1.0) / 2.0
        interp = np.ones((8, 8))
        for col_at in range(8):
            for other_at in range(8):
                if other_at != col_at:
                    interp[:, col_at] *= (targets - points[other_at]) / (points[col_at] - points[other_at])
        halves.append(interp)
        projections.append(0.5 * (interp.T * weights[None, :]) / weights[:, None])
    interp_mats = np.stack([np.kron(halves[first_at], halves[second_at]) for first_at in range(2) for second_at in range(2)] + [np.eye(64)])
    proj_mats = np.stack([np.kron(projections[first_at], projections[second_at]) for first_at in range(2) for second_at in range(2)] + [np.eye(64)])
    perm_table = np.zeros((8, 64), np.int32)
    for orient_code in range(8):
        for first_at in range(8):
            for second_at in range(8):
                if orient_code & 4:
                    upper_at, lower_at = second_at, first_at
                else:
                    upper_at, lower_at = first_at, second_at
                if orient_code & 1:
                    upper_at = 7 - upper_at
                if orient_code & 2:
                    lower_at = 7 - lower_at
                perm_table[orient_code, 8 * first_at + second_at] = 8 * upper_at + lower_at
    inverse_table = np.argsort(perm_table, axis=1).astype(np.int32)
    across_y = np.kron(np.eye(2), np.kron(deriv_mat, np.eye(8)))
    along_z = np.kron(np.eye(2), np.kron(np.eye(8), deriv_mat))
    lift_end = float(1.0 / weights[0])
    return (jnp.asarray(deriv_mat, jnp.float32), jnp.asarray(interp_mats, jnp.float32), jnp.asarray(proj_mats, jnp.float32),
            jnp.asarray(perm_table, jnp.int32), jnp.asarray(inverse_table, jnp.int32), lift_end,
            jnp.asarray(across_y, jnp.float32), jnp.asarray(along_z, jnp.float32))


def face_traces(current):
    fields, elements, npoints = current.shape
    cube_vals = current.reshape(fields, elements, 8, 8, 8)
    stacked = jnp.stack([cube_vals[:, :, 0], cube_vals[:, :, 7], cube_vals[:, :, :, 0], cube_vals[:, :, :, 7],
                         cube_vals[:, :, :, :, 0], cube_vals[:, :, :, :, 7]], axis=2)
    return stacked.reshape(fields, elements * 6, 64)


def spread_faces(jump_term, elements):
    fields = jump_term.shape[0]
    face_vals = jump_term.reshape(fields, elements, 6, 8, 8)
    cube_vals = jnp.zeros((fields, elements, 8, 8, 8), jnp.float32)
    cube_vals = cube_vals.at[:, :, 0].add(face_vals[:, :, 0])
    cube_vals = cube_vals.at[:, :, 7].add(face_vals[:, :, 1])
    cube_vals = cube_vals.at[:, :, :, 0].add(face_vals[:, :, 2])
    cube_vals = cube_vals.at[:, :, :, 7].add(face_vals[:, :, 3])
    cube_vals = cube_vals.at[:, :, :, :, 0].add(face_vals[:, :, 4])
    cube_vals = cube_vals.at[:, :, :, :, 7].add(face_vals[:, :, 5])
    return cube_vals.reshape(fields, elements, 512)


def dim_picks(face_ids):
    return (((face_ids % 6) // 2)[None, :] == jnp.arange(3, dtype=jnp.int32)[:, None]).astype(jnp.float32)


def normal_flux(trace_set, face_ids):
    pick_mask = dim_picks(face_ids)
    sign_vals = ((face_ids % 2) * 2 - 1).astype(jnp.float32)[:, None]
    normal_vel = jnp.sum(pick_mask[:, :, None] * trace_set[1:4], axis=0)
    pressure = sign_vals * trace_set[4]
    return jnp.stack([sign_vals * normal_vel, pick_mask[0][:, None] * pressure, pick_mask[1][:, None] * pressure,
                      pick_mask[2][:, None] * pressure, sign_vals * normal_vel])


def wall_state(own_side, face_ids):
    flip_vals = 1.0 - 2.0 * dim_picks(face_ids)
    return jnp.concatenate([own_side[:1], own_side[1:4] * flip_vals[:, :, None], own_side[4:]], axis=0)


def rusanov(own_side, other_side, face_ids):
    average = 0.5 * (normal_flux(own_side, face_ids) + normal_flux(other_side, face_ids))
    return average - 0.5 * wave_speed * (other_side - own_side)


def orient(values, orient_codes, lookup):
    matches = (orient_codes[:, None] == jnp.arange(8, dtype=jnp.int32)[None, :]).astype(jnp.int32)
    gather_index = jnp.sum(matches[:, :, None] * lookup[None, :, :], axis=1)
    return jnp.take_along_axis(values, jnp.broadcast_to(gather_index[None], values.shape), axis=2)


def child_apply(values, child_ids, matrices):
    mapped = jnp.einsum('fnj,cij->cfni', values, matrices, precision=highest)
    pick_mask = (child_ids[None, :] == jnp.arange(5, dtype=jnp.int32)[:, None]).astype(jnp.float32)
    return jnp.sum(pick_mask[:, None, :, None] * mapped, axis=0)


def volume_term(current, deriv_mat):
    fields, elements, npoints = current.shape
    cube_vals = current.reshape(fields, elements, 8, 8, 8)
    grad_x = jnp.einsum('im,femjk->feijk', deriv_mat, cube_vals[1:5:3], precision=highest).reshape(2, elements, 512)
    grad_y = jnp.einsum('jm,feimk->feijk', deriv_mat, cube_vals[2:5:2], precision=highest).reshape(2, elements, 512)
    grad_z = jnp.einsum('km,feijm->feijk', deriv_mat, cube_vals[3:5], precision=highest).reshape(2, elements, 512)
    diverge = grad_x[0] + grad_y[0] + grad_z[0]
    return -jnp.stack([diverge, grad_x[1], grad_y[1], grad_z[1], diverge])


def reference(state, levels, send_faces, send_counts, recv_faces, recv_orients, recv_counts, curve_faces, curve_orients, curve_counts):
    deriv_mat, interp_mats, proj_mats, perm_table, inverse_table, lift_end, across_y, along_z = basis_tables()
    fields, elements, npoints = state.shape
    face_total = elements * 6
    offsets = (jnp.arange(N_CURVE * N_TILE, dtype=jnp.int32) * (6 * E_DEV)).reshape(N_CURVE, N_TILE)
    scales = jnp.exp2(levels.astype(jnp.float32))
    face_scales = jnp.repeat(scales, 6) * lift_end
    slot_range = jnp.arange(CAPM, dtype=jnp.int32)
    send_grid = send_faces.reshape(N_CURVE, N_TILE, N_TILE, CAPM)
    send_live = slot_range < send_counts.reshape(N_CURVE, N_TILE, N_TILE)[..., None]
    send_ids = jnp.where(send_live, offsets[:, :, None, None] + send_grid // 5, face_total).reshape(-1).astype(jnp.int32)
    child_ids = (send_grid % 5).reshape(-1).astype(jnp.int32)
    send_mask = send_live.reshape(-1).astype(jnp.float32)[None, :, None]
    recv_grid = recv_faces.reshape(N_CURVE, N_TILE, N_TILE, CAPM)
    recv_live = slot_range < recv_counts.reshape(N_CURVE, N_TILE, N_TILE)[..., None]
    recv_ids = jnp.where(recv_live, offsets[:, :, None, None] + recv_grid, face_total).reshape(-1).astype(jnp.int32)
    recv_codes = recv_orients.reshape(-1).astype(jnp.int32)
    recv_mask = recv_live.reshape(-1).astype(jnp.float32)[None, :, None]
    rim_range = jnp.arange(CAPH, dtype=jnp.int32)
    curve_grid = curve_faces.reshape(N_CURVE, N_TILE, 2, CAPH)
    curve_live = rim_range < curve_counts.reshape(N_CURVE, N_TILE, 2)[..., None]
    curve_ids = jnp.where(curve_live, offsets[:, :, None, None] + curve_grid, face_total).reshape(-1).astype(jnp.int32)
    curve_codes = curve_orients.reshape(-1).astype(jnp.int32)
    curve_mask = curve_live.reshape(-1).astype(jnp.float32)[None, :, None]
    all_faces = jnp.arange(face_total, dtype=jnp.int32)
    slot_shape = (fields, N_CURVE, N_TILE, N_TILE, CAPM, 64)

    def rhs(current):
        traces = face_traces(current)
        padded = jnp.concatenate([traces, jnp.zeros((fields, 1, 64), jnp.float32)], axis=1)
        mortar = child_apply(padded[:, send_ids], child_ids, interp_mats) * send_mask
        arrived = jnp.transpose(mortar.reshape(slot_shape), (0, 1, 3, 2, 4, 5)).reshape(fields, -1, 64)
        fine_flux = rusanov(padded[:, recv_ids], orient(arrived, recv_codes, perm_table), recv_ids) * recv_mask
        returned = orient(fine_flux, recv_codes, inverse_table)
        coarse_flux = -jnp.transpose(returned.reshape(slot_shape), (0, 1, 3, 2, 4, 5)).reshape(fields, -1, 64) * send_mask
        own_curve = padded[:, curve_ids].reshape(fields, N_CURVE, N_TILE, 2, CAPH, 64)
        empty_rim = jnp.zeros((fields, 1, N_TILE, CAPH, 64), jnp.float32)
        from_left = jnp.concatenate([empty_rim, own_curve[:, :-1, :, 1]], axis=1)
        from_right = jnp.concatenate([own_curve[:, 1:, :, 0], empty_rim], axis=1)
        neighbours = jnp.stack([from_left, from_right], axis=3).reshape(fields, -1, 64)
        curve_flux = rusanov(own_curve.reshape(fields, -1, 64), orient(neighbours, curve_codes, perm_table), curve_ids) * curve_mask
        accumulated = jnp.zeros((fields, face_total + 1, 64), jnp.float32)
        accumulated = accumulated.at[:, send_ids].add(child_apply(coarse_flux, child_ids, proj_mats))
        accumulated = accumulated.at[:, recv_ids].add(fine_flux)
        accumulated = accumulated.at[:, curve_ids].add(curve_flux)
        listed = jnp.zeros((face_total + 1,), jnp.float32)
        listed = listed.at[send_ids].add(1.0).at[recv_ids].add(1.0).at[curve_ids].add(1.0)
        wall_flux = rusanov(traces, wall_state(traces, all_faces), all_faces)
        flux_star = jnp.where(listed[None, :face_total, None] > 0.0, accumulated[:, :face_total], wall_flux)
        jump_term = (normal_flux(traces, all_faces) - flux_star) * face_scales[None, :, None]
        return volume_term(current, deriv_mat) * scales[None, :, None] + spread_faces(jump_term, elements)

    section_one = state + time_step * rhs(state)
    section_two = 0.75 * state + 0.25 * (section_one + time_step * rhs(section_one))
    return state / 3.0 + (2.0 / 3.0) * (section_two + time_step * rhs(section_two))
```

```python
import jax
import jax.numpy as jnp
import numpy as np
from jax import lax
from jax.experimental import pallas as pl
from jax.experimental.pallas import tpu as pltpu
from jax.sharding import PartitionSpec as P


time_step = 0.002
inner_nodes = [
    -0.8717401485096066,
    -0.5917001814331423,
    -0.20929921790247888,
    0.20929921790247888,
    0.5917001814331423,
    0.8717401485096066,
]
f32, bf16, i32 = jnp.float32, jnp.bfloat16, jnp.int32

PERM, INV, PICK, SPREAD, INDEX_ROWS = 0, 128, 256, 288, 416
CHILD, SEND_Z, RECV_Z, RECV_LIVE, CURVE_LIVE = 0, 8, 16, 24, 32


def legendre_seven(abscissa):
    before = abscissa * 0.0 + 1.0
    current = abscissa + 0.0
    for order in range(1, 7):
        before, current = (
            current,
            ((2 * order + 1) * abscissa * current - order * before) / (order + 1),
        )
    return current


def split_np(array):
    array = np.asarray(array, np.float32).astype(np.float64)
    high = array.astype(bf16).astype(np.float64)
    low = (array - high).astype(bf16).astype(np.float64)
    return high, low


def tables():
    degree = 7
    points = np.array([-1.0] + inner_nodes + [1.0])
    values = legendre_seven(points)
    weights = 2.0 / (degree * (degree + 1) * values**2)
    deriv = np.zeros((8, 8))
    for i in range(8):
        for m in range(8):
            if i != m:
                deriv[i, m] = values[i] / (values[m] * (points[i] - points[m]))
    deriv[0, 0] = -degree * (degree + 1) / 4.0
    deriv[7, 7] = degree * (degree + 1) / 4.0
    weak = -deriv
    weak[0, 0] -= 28.0
    weak[7, 7] += 28.0
    halves, projections = [], []
    for side in range(2):
        targets = (points + 2.0 * side - 1.0) / 2.0
        interp = np.ones((8, 8))
        for m in range(8):
            for other in range(8):
                if other != m:
                    interp[:, m] *= (targets - points[other]) / (points[m] - points[other])
        halves.append(interp)
        projections.append(0.5 * (interp.T * weights[None, :]) / weights[:, None])

    def child_weights(parts):
        columns = [
            np.kron(np.eye(2), np.kron(parts[a], parts[b]).T) for a in range(2) for b in range(2)
        ]
        high, low = split_np(np.concatenate(columns, axis=1))
        return np.concatenate([high, high, low], axis=0)

    def tile_weights(matrix):
        high, low = split_np(matrix.T)
        return np.block([[high, low], [high, np.zeros_like(high)]])

    along_y = np.kron(np.eye(2), np.kron(weak, np.eye(8)))
    along_z = np.kron(np.eye(16), weak)
    derivs = np.concatenate([tile_weights(along_y), tile_weights(along_z)], axis=1)
    mats = np.concatenate([child_weights(halves), child_weights(projections), derivs], axis=0)
    coefs = np.zeros((32, 128))
    for a in range(4):
        for b in range(4):
            coefs[a * 4 + b, :64] = weak[2 * a, 2 * b]
            coefs[a * 4 + b, 64:] = weak[2 * a + 1, 2 * b + 1]
            coefs[16 + a * 4 + b, :64] = weak[2 * a, 2 * b + 1]
            coefs[16 + a * 4 + b, 64:] = weak[2 * a + 1, 2 * b]

    perm = np.zeros((8, 64), np.int64)
    for code in range(8):
        for s in range(8):
            for t in range(8):
                a, c = (t, s) if code & 4 else (s, t)
                a = 7 - a if code & 1 else a
                c = 7 - c if code & 2 else c
                perm[code, 8 * s + t] = 8 * a + c
    inverse = np.argsort(perm, axis=1)
    lane = np.arange(128)
    rows = []
    for table in (perm, inverse):
        for half in range(2):
            for code in range(8):
                rows.append(table[code][lane % 64] + 64 * half)
    slot_lane = lane % 64
    i, rest = slot_lane // 8, slot_lane % 8
    for end in (7, 0):
        rows.append(64 * (i % 2) + 8 * end + rest)
        rows.append(64 * (i % 2) + 8 * rest + end)
    for kind in range(2):
        for half in range(2):
            for tile in range(4):
                first = 2 * tile + lane // 64
                second = lane % 8 if kind == 0 else (lane // 8) % 8
                rows.append(8 * first + second + 64 * half)
    index = np.repeat(np.stack(rows), 8, axis=0)
    return (
        jnp.asarray(index, i32),
        jnp.asarray(mats, f32).astype(bf16),
        jnp.asarray(coefs, f32),
    )


def take(values, index):
    return jnp.take_along_axis(values, index, axis=1, mode="promise_in_bounds")


def lanes():
    return lax.broadcasted_iota(i32, (8, 128), 1)


def split(values):
    high = values.astype(bf16)
    return high, (values - high.astype(f32)).astype(bf16)


def row(ref, start):
    return ref[pl.ds(pl.multiple_of(start, 8), 8), :]


def child_map(pieces, mats_ref, start, codes):
    high, low = split(jnp.concatenate(pieces, axis=0))
    mapped = jnp.dot(
        jnp.concatenate([high, low, high], axis=1),
        mats_ref[start : start + 384, :],
        preferred_element_type=f32,
    )
    out = []
    for f, piece in enumerate(pieces):
        total = jnp.where(codes == 4, piece, 0.0)
        for c in range(4):
            total = jnp.where(codes == c, mapped[8 * f : 8 * f + 8, 128 * c : 128 * c + 128], total)
        out.append(total)
    return out


def neighbour_part(q, sign, is_z, scale):
    normal = jnp.where(is_z, q[3], q[2]) * sign
    push = q[4] * sign
    return [
        (normal - q[0]) * scale,
        q[1] * -scale,
        (jnp.where(is_z, 0.0, push) - q[2]) * scale,
        (jnp.where(is_z, push, 0.0) - q[3]) * scale,
        (normal - q[4]) * scale,
    ]


def pack_curve(u_ref, slots, masks_ref, index_ref, tmp, left_ref, right_ref):
    low = lanes() < 64
    for side, out_ref, sign in ((0, left_ref, 1.0), (1, right_ref, -1.0)):
        for k in range(8):
            picked = []
            for s in (16 * side + k, 16 * side + k + 8):
                trace = row(u_ref, slots[s] + 768 * side)
                picked.append(take(trace, row(index_ref, slots[64 + s] + INV + 64 * side)))
            tmp[64 * side + 8 * k : 64 * side + 8 * k + 8, :] = jnp.where(low, *picked)
        q = [tmp[pl.ds(64 * side + f, 8, stride=8), :] for f in range(5)]
        scale = masks_ref[CURVE_LIVE + 8 * side : CURVE_LIVE + 8 * side + 8, :] * 14.0
        parts = [
            (sign * q[1] - q[0]) * scale,
            (sign * q[4] - q[1]) * scale,
            q[2] * -scale,
            q[3] * -scale,
            (sign * q[1] - q[4]) * scale,
        ]
        for f in range(5):
            out_ref[pl.ds(f, 8, stride=8), :] = parts[f]


def pack_tile(u_ref, slots, masks_ref, index_ref, mats_ref, tmp, own_ref, tile_ref):
    low = lanes() < 64
    quarter = (lanes() % 64) // 16
    for side in range(2):
        for p in range(8):
            picked = []
            for k in range(2):
                s = 32 + 16 * side + 2 * p + k
                index = row(index_ref, slots[128 + s] * 8 + PICK + 16 * side)
                trace = take(row(u_ref, slots[s]), index)
                for a in range(1, 4):
                    other = take(row(u_ref, slots[s] + 256 * a), index)
                    trace = jnp.where(quarter == a, other, trace)
                picked.append(trace)
            pair = jnp.where(low, *picked)
            if side == 1:
                s = 48 + 2 * p
                pair = jnp.where(
                    low,
                    take(pair, row(index_ref, slots[64 + s] + INV)),
                    take(pair, row(index_ref, slots[65 + s] + INV + 64)),
                )
            tmp[64 * side + 8 * p : 64 * side + 8 * p + 8, :] = pair
    q = [tmp[pl.ds(f, 8, stride=8), :] for f in range(5)]
    q = child_map(q, mats_ref, 0, masks_ref[CHILD : CHILD + 8, :])
    is_z = masks_ref[SEND_Z : SEND_Z + 8, :] > 0.0
    for f, part in enumerate(neighbour_part(q, -1.0, is_z, 14.0)):
        tile_ref[pl.ds(f, 8, stride=16), :] = part
        own_ref[pl.ds(f, 8, stride=8), :] = part
    q = [tmp[pl.ds(64 + f, 8, stride=8), :] for f in range(5)]
    is_z = masks_ref[RECV_Z : RECV_Z + 8, :] > 0.0
    scale = masks_ref[RECV_LIVE : RECV_LIVE + 8, :] * 14.0
    for f, part in enumerate(neighbour_part(q, 1.0, is_z, scale)):
        tile_ref[pl.ds(8 + f, 8, stride=16), :] = part


def spread(w_ref, pair, slots, s, half, end, index_ref):
    kind = slots[128 + s]
    lane = lanes()
    position = jnp.where(kind == 0, (lane // 8) % 8, lane % 8)
    at_face = position == end
    for a in range(4):
        moved = take(pair, row(index_ref, kind * 64 + SPREAD + 32 * half + 8 * a))
        block = pl.ds(pl.multiple_of(slots[s] + 256 * a, 8), 8)
        w_ref[block, :] = w_ref[block, :] - jnp.where(at_face, moved, 0.0)


def unpack(w_ref, slots, masks_ref, index_ref, mats_ref, tmp, from_left, from_right, tile_ref, own_ref):
    low = lanes() < 64
    q = [
        tile_ref[pl.ds(8 + f, 8, stride=16), :] - own_ref[pl.ds(f, 8, stride=8), :]
        for f in range(5)
    ]
    q = child_map(q, mats_ref, 384, masks_ref[CHILD : CHILD + 8, :])
    for f in range(5):
        tmp[pl.ds(f, 8, stride=8), :] = q[f]
    for side, in_ref in ((0, from_left), (1, from_right)):
        for k in range(8):
            pair = in_ref[8 * k : 8 * k + 8, :]
            turned = pltpu.roll(pair, 64, 1)
            for s, value in ((k, (pair, turned)[side]), (k + 8, (turned, pair)[side])):
                block = pl.ds(pl.multiple_of(slots[16 * side + s] + 768 * side, 8), 8)
                kept = jnp.where(low, value, 0.0) if side == 0 else jnp.where(low, 0.0, value)
                w_ref[block, :] = w_ref[block, :] - kept
    for p in range(8):
        s = 48 + 2 * p
        pair = tile_ref[16 * p : 16 * p + 8, :]
        pair = jnp.where(
            low,
            take(pair, row(index_ref, slots[64 + s] + PERM)),
            take(pair, row(index_ref, slots[65 + s] + PERM + 64)),
        )
        for k in range(2):
            spread(w_ref, pair, slots, s + k, k, 0, index_ref)
    for p in range(8):
        pair = tmp[8 * p : 8 * p + 8, :]
        for k in range(2):
            spread(w_ref, pair, slots, 32 + 2 * p + k, k, 7, index_ref)


def inside(u_ref, faces_ref, mats_ref, coefs_ref, w_ref):
    fields = [[u_ref[pl.ds(256 * a + f, 32, stride=8), :] for a in range(4)] for f in range(5)]
    dens, vx, vy, vz, pres = fields

    def along(vel, start):
        stacked = [values[a] for values in (vel, pres) for a in range(4)]
        high, low = split(jnp.concatenate(stacked, axis=0))
        both = jnp.dot(
            jnp.concatenate([high, low], axis=1),
            mats_ref[768:1024, start : start + 256],
            preferred_element_type=f32,
        )
        both = both[:, :128] + both[:, 128:]
        return [both[32 * n : 32 * n + 32] for n in range(8)]

    grad_y = along(vy, 0)
    grad_z = along(vz, 256)
    grad_x = []
    for values in (vx, pres):
        plain = values
        turned = [pltpu.roll(t, 64, 1) for t in plain]
        for a in range(4):
            total = None
            for b in range(4):
                n = 4 * a + b
                term = plain[b] * coefs_ref[n : n + 1, :] + turned[b] * coefs_ref[16 + n : 17 + n, :]
                total = term if total is None else total + term
            grad_x.append(total)
    face = [faces_ref[32 * n : 32 * n + 32, :] for n in range(11)]
    ay, az, ayz, ax0, ux0, ax3, ux3, uy0, uy7, uz0, uz7 = face
    for a in range(4):
        d, x, y, z, p = (values[a] for values in fields)
        asum = ayz
        inward = -(ay * y + az * z)
        if a == 0:
            asum = asum + ax0
            inward = inward - ax0 * x
        elif a == 3:
            asum = asum + ax3
            inward = inward + ax3 * x
        diverge = grad_x[a] + grad_y[a] + grad_z[a] - inward
        out = [diverge - asum * d, grad_x[4 + a] - ayz * x, None, None, diverge - asum * p]
        if a == 0:
            out[1] = out[1] + ux0 * (p - x)
        elif a == 3:
            out[1] = out[1] - ux3 * (p + x)
        out[2] = grad_y[4 + a] + uy0 * (p - y) - uy7 * (p + y) - (asum - ay) * y
        out[3] = grad_z[4 + a] + uz0 * (p - z) - uz7 * (p + z) - (asum - az) * z
        for f in range(5):
            w_ref[pl.ds(256 * a + f, 32, stride=8), :] = out[f]


def first_kernel(
    state_hbm, levels_hbm, send_faces_hbm, send_counts_hbm, recv_faces_hbm, recv_orients_hbm,
    recv_counts_hbm, curve_faces_hbm, curve_orients_hbm, curve_counts_hbm, index_hbm, mats_hbm,
    u_ref, left_ref, right_ref, own_ref, tile_hbm, slots, masks_ref,
    levels, send_faces, send_counts, recv_faces, recv_orients, recv_counts, curve_faces,
    curve_orients, curve_counts, state_ref, index_ref, mats_ref, tmp, tile_ref, sems,
):
    numbers = [
        pltpu.make_async_copy(source, target, sems.at[n])
        for n, (source, target) in enumerate(
            (
                (curve_faces_hbm, curve_faces),
                (curve_orients_hbm, curve_orients),
                (curve_counts_hbm, curve_counts),
                (send_faces_hbm, send_faces),
                (send_counts_hbm, send_counts),
                (recv_faces_hbm, recv_faces),
                (recv_orients_hbm, recv_orients),
                (recv_counts_hbm, recv_counts),
                (levels_hbm, levels),
            )
        )
    ]
    arrays = [
        pltpu.make_async_copy(source, target, sems.at[9 + n])
        for n, (source, target) in enumerate(
            (
                (state_hbm, state_ref),
                (index_hbm, index_ref),
                (mats_hbm.at[pl.ds(0, 384), :], mats_ref),
            )
        )
    ]
    for copy in numbers + arrays:
        copy.start()
    for copy in numbers:
        copy.wait()
    low = lax.broadcasted_iota(i32, (1, 128), 1) < 64

    def halves(a, b):
        return jnp.where(low, a, b)

    for side in range(2):
        live = []
        for k in range(16):
            s = 16 * side + k
            is_live = k < curve_counts[side]
            element = (curve_faces[side, k] * 10923) >> 16
            slots[s] = element * 8
            slots[64 + s] = curve_orients[side, k] * 8
            slots[128 + s] = 0
            slots[192 + s] = jnp.where(is_live, 32 * side + element, 192)
            live.append(jnp.where(is_live, 1.0, 0.0))
        for k in range(8):
            at = CURVE_LIVE + 8 * side + k
            masks_ref[at : at + 1, :] = halves(live[k], live[k + 8])
    for p in range(8):
        child, kinds, recv_kinds, recv_live = [], [], [], []
        for k in range(2):
            s = 32 + 2 * p + k
            number = send_faces[k, p]
            is_live = k < send_counts[p]
            element = (number * 2185) >> 16
            rest = number - 30 * element
            is_z = rest >= 25
            slots[s] = element * 8
            slots[64 + s] = 0
            slots[128 + s] = jnp.where(is_z, 1, 0)
            slots[192 + s] = jnp.where(is_live, jnp.where(is_z, 160, 96) + element, 192)
            child.append(jnp.where(is_live, jnp.where(is_z, rest - 25, rest - 15), -1))
            kinds.append(jnp.where(is_z, 1.0, 0.0))
            s = 48 + 2 * p + k
            number = recv_faces[k, p]
            is_live = k < recv_counts[p]
            element = (number * 10923) >> 16
            is_z = number - 6 * element == 4
            slots[s] = element * 8
            slots[64 + s] = recv_orients[k, p] * 8
            slots[128 + s] = jnp.where(is_z, 1, 0)
            slots[192 + s] = jnp.where(is_live, jnp.where(is_z, 128, 64) + element, 192)
            recv_kinds.append(jnp.where(is_z, 1.0, 0.0))
            recv_live.append(jnp.where(is_live, 1.0, 0.0))
        masks_ref[CHILD + p : CHILD + p + 1, :] = halves(*child).astype(f32)
        masks_ref[SEND_Z + p : SEND_Z + p + 1, :] = halves(*kinds)
        masks_ref[RECV_Z + p : RECV_Z + p + 1, :] = halves(*recv_kinds)
        masks_ref[RECV_LIVE + p : RECV_LIVE + p + 1, :] = halves(*recv_live)
    for e in range(32):
        slots[256 + e] = 1 << levels[e]
    for copy in arrays:
        copy.wait()
    for f in range(5):
        for a in range(4):
            u_ref[pl.ds(256 * a + f, 32, stride=8), :] = state_ref[f, :, 128 * a : 128 * a + 128]
    pack_tile(u_ref, slots, masks_ref, index_ref, mats_ref, tmp, own_ref, tile_ref)
    send = pltpu.make_async_copy(tile_ref, tile_hbm, sems.at[12])
    send.start()
    pack_curve(u_ref, slots, masks_ref, index_ref, tmp, left_ref, right_ref)
    send.wait()


def faces_kernel(slots, faces_ref, scale_ref, listed):
    listed[...] = jnp.zeros_like(listed)
    for s in range(64):
        listed[pl.ds(slots[192 + s], 1), :] = jnp.ones((1, 128), f32)
    for e in range(32):
        scale_ref[8 * e : 8 * e + 8, :] = (
            jnp.full((8, 128), slots[256 + e], i32).astype(f32) * time_step
        )
    lane = lax.broadcasted_iota(i32, (32, 128), 1)
    on = [listed[32 * f : 32 * f + 32, :] for f in range(6)]
    where_0 = [lane < 64, (lane // 8) % 8 == 0, lane % 8 == 0]
    where_7 = [lane >= 64, (lane // 8) % 8 == 7, lane % 8 == 7]

    def keep(test, values):
        return jnp.where(test, values, 0.0)

    ay = keep(where_0[1], 14.0 * on[2])
    az = keep(where_0[2], 14.0 * on[4])
    values = [
        ay,
        az,
        ay + az,
        keep(where_0[0], 14.0 * on[0]),
        keep(where_0[0], 28.0 - 14.0 * on[0]),
        keep(where_7[0], 14.0 * on[1]),
        keep(where_7[0], 28.0 - 14.0 * on[1]),
        keep(where_0[1], 28.0 - 14.0 * on[2]),
        keep(where_7[1], 28.0 - 28.0 * on[3]),
        keep(where_0[2], 28.0 - 14.0 * on[4]),
        keep(where_7[2], 28.0 - 28.0 * on[5]),
    ]
    for n, value in enumerate(values):
        faces_ref[32 * n : 32 * n + 32, :] = value


def next_kernel(
    slots_any, u_ref, from_left, from_right, arrived_ref, sent_ref, masks_ref, faces_ref, scale_ref,
    index_ref, mats_ref, coefs_ref,
    out_ref, left_ref, right_ref, own_ref, tile_hbm, w_ref, tmp, slots, tile_ref, sems,
):
    fetch = pltpu.make_async_copy(slots_any, slots, sems.at[0])
    fetch.start()
    inside(u_ref, faces_ref, mats_ref, coefs_ref, w_ref)
    fetch.wait()
    unpack(
        w_ref, slots, masks_ref, index_ref, mats_ref, tmp, from_left, from_right, arrived_ref, sent_ref
    )
    for a in range(4):
        out_ref[256 * a : 256 * a + 256, :] = w_ref[256 * a : 256 * a + 256, :] * scale_ref[...]
    pack_tile(out_ref, slots, masks_ref, index_ref, mats_ref, tmp, own_ref, tile_ref)
    send = pltpu.make_async_copy(tile_ref, tile_hbm, sems.at[1])
    send.start()
    pack_curve(out_ref, slots, masks_ref, index_ref, tmp, left_ref, right_ref)
    send.wait()


def last_kernel(
    slots_any, u_ref, from_left, from_right, arrived_ref, sent_ref, masks_ref, faces_ref, scale_ref,
    index_ref, mats_ref, coefs_ref, state_ref, first_ref,
    out_ref, w_ref, tmp, slots, sems,
):
    fetch = pltpu.make_async_copy(slots_any, slots, sems.at[0])
    fetch.start()
    inside(u_ref, faces_ref, mats_ref, coefs_ref, w_ref)
    fetch.wait()
    unpack(
        w_ref, slots, masks_ref, index_ref, mats_ref, tmp, from_left, from_right, arrived_ref, sent_ref
    )
    scale = scale_ref[pl.ds(0, 32, stride=8), :] * (1.0 / 6.0)
    for f in range(5):
        for a in range(4):
            at = (pl.ds(256 * a + f, 32, stride=8), slice(None))
            column = slice(128 * a, 128 * a + 128)
            out_ref[f, :, column] = (
                state_ref[f, :, column] + first_ref[at] + 0.5 * u_ref[at] + w_ref[at] * scale
            )


def shards(
    state, levels, send_faces, send_counts, recv_faces, recv_orients, recv_counts,
    curve_faces, curve_orients, curve_counts,
):
    index, mats, coefs = tables()
    vmem = pl.BlockSpec(memory_space=pltpu.VMEM)
    smem = pl.BlockSpec(memory_space=pltpu.SMEM)
    hbm = pl.BlockSpec(memory_space=pltpu.HBM)
    anywhere = pl.BlockSpec(memory_space=pl.ANY)

    def shape(*dims, kind=f32):
        return jax.ShapeDtypeStruct(dims, kind)

    def call(kernel, name, **kwargs):
        return pl.pallas_call(
            kernel,
            name=name,
            compiler_params=pltpu.CompilerParams(vmem_limit_bytes=16 * 1024 * 1024),
            **kwargs,
        )

    payload = [shape(64, 128)] * 3 + [shape(128, 128)]
    n_curve = lax.axis_size("curve")
    rightward = [(i, i + 1) for i in range(n_curve - 1)]
    leftward = [(i + 1, i) for i in range(n_curve - 1)]

    def exchange(left, right, tile):
        arrived = lax.all_to_all(
            tile.reshape(8, 16, 128), "tile", split_axis=0, concat_axis=0, tiled=True
        )
        from_left = lax.ppermute(right, "curve", rightward)
        from_right = lax.ppermute(left, "curve", leftward)
        return from_left, from_right, arrived.reshape(128, 128)

    numbers = [
        levels, send_faces.T, send_counts, recv_faces.T, recv_orients.T, recv_counts,
        curve_faces, curve_orients, curve_counts,
    ]
    u, left, right, own, tile, slots, masks = call(
        first_kernel,
        "first",
        out_shape=[shape(1024, 128), *payload, shape(288, kind=i32), shape(48, 128)],
        in_specs=[hbm] * 12,
        out_specs=[vmem] * 4 + [hbm, smem, vmem],
        scratch_shapes=[pltpu.SMEM(x.shape, i32) for x in numbers]
        + [
            pltpu.VMEM(state.shape, f32),
            pltpu.VMEM(index.shape, i32),
            pltpu.VMEM((384, 512), bf16),
            pltpu.VMEM((128, 128), f32),
            pltpu.VMEM((128, 128), f32),
            pltpu.SemaphoreType.DMA((13,)),
        ],
    )(*[pltpu.with_memory_space_constraint(x, pltpu.HBM) for x in (state, *numbers, index, mats)])
    scratch = [pltpu.VMEM((1024, 128), f32), pltpu.VMEM((128, 128), f32), pltpu.SMEM((288,), i32)]
    sems = pltpu.SemaphoreType.DMA((2,))
    kept = []
    for section in range(3):
        from_left, from_right, arrived = exchange(left, right, tile)
        if section == 0:
            faces, scale = call(
                faces_kernel,
                "faces",
                out_shape=[shape(352, 128), shape(256, 128)],
                in_specs=[smem],
                out_specs=[vmem] * 2,
                scratch_shapes=[pltpu.VMEM((200, 128), f32)],
                cost_estimate=pl.CostEstimate(
                    flops=20_000_000, bytes_accessed=1_000_000, transcendentals=0
                ),
            )(slots)
        args = (
            slots, u, from_left, from_right, arrived, own, masks, faces, scale,
            index, mats, coefs,
        )
        if section < 2:
            u, left, right, own, tile = call(
                next_kernel,
                "next",
                out_shape=[shape(1024, 128), *payload],
                in_specs=[anywhere] + [vmem] * 11,
                out_specs=[vmem] * 4 + [hbm],
                scratch_shapes=[*scratch, pltpu.VMEM((128, 128), f32), sems],
            )(*args)
            kept.append(u)
    return call(
        last_kernel,
        "last",
        out_shape=shape(5, 32, 512),
        in_specs=[anywhere] + [vmem] * 13,
        out_specs=vmem,
        scratch_shapes=[*scratch, sems],
    )(*args, state, kept[0])


def solution(mesh):
    both = P(("curve", "tile"))
    rows = P(("curve", "tile"), None)
    return jax.shard_map(
        shards,
        mesh=mesh,
        in_specs=(P(None, ("curve", "tile"), None), both, rows, both, rows, rows, both, rows, rows, both),
        out_specs=P(None, ("curve", "tile"), None),
        check_vma=False,
    )
```

```python
import jax
import jax.numpy as jnp
import numpy as np
from jax import lax
from jax.experimental import pallas as pl
from jax.experimental.pallas import tpu as pltpu
from jax.sharding import PartitionSpec as P


time_step = 0.002
inner_nodes = [
    -0.8717401485096066,
    -0.5917001814331423,
    -0.20929921790247888,
    0.20929921790247888,
    0.5917001814331423,
    0.8717401485096066,
]
f32, bf16, i32 = jnp.float32, jnp.bfloat16, jnp.int32

PERM, INV, PICK, SPREAD, INDEX_ROWS = 0, 128, 256, 288, 416
CHILD, SEND_Z, RECV_Z, RECV_LIVE, CURVE_LIVE = 0, 8, 16, 24, 32


def legendre_seven(abscissa):
    before = abscissa * 0.0 + 1.0
    current = abscissa + 0.0
    for order in range(1, 7):
        before, current = (
            current,
            ((2 * order + 1) * abscissa * current - order * before) / (order + 1),
        )
    return current


def split_np(array):
    array = np.asarray(array, np.float32).astype(np.float64)
    high = array.astype(bf16).astype(np.float64)
    low = (array - high).astype(bf16).astype(np.float64)
    return high, low


def tables():
    degree = 7
    points = np.array([-1.0] + inner_nodes + [1.0])
    values = legendre_seven(points)
    weights = 2.0 / (degree * (degree + 1) * values**2)
    deriv = np.zeros((8, 8))
    for i in range(8):
        for m in range(8):
            if i != m:
                deriv[i, m] = values[i] / (values[m] * (points[i] - points[m]))
    deriv[0, 0] = -degree * (degree + 1) / 4.0
    deriv[7, 7] = degree * (degree + 1) / 4.0
    weak = -deriv
    weak[0, 0] -= 28.0
    weak[7, 7] += 28.0
    halves, projections = [], []
    for side in range(2):
        targets = (points + 2.0 * side - 1.0) / 2.0
        interp = np.ones((8, 8))
        for m in range(8):
            for other in range(8):
                if other != m:
                    interp[:, m] *= (targets - points[other]) / (points[m] - points[other])
        halves.append(interp)
        projections.append(0.5 * (interp.T * weights[None, :]) / weights[:, None])

    def child_weights(parts):
        columns = [
            np.kron(np.eye(2), np.kron(parts[a], parts[b]).T) for a in range(2) for b in range(2)
        ]
        high, low = split_np(np.concatenate(columns, axis=1))
        return np.concatenate([high, high, low], axis=0)

    def tile_weights(matrix):
        high, low = split_np(matrix.T)
        return np.block([[high, low], [high, np.zeros_like(high)]])

    along_y = np.kron(np.eye(2), np.kron(weak, np.eye(8)))
    along_z = np.kron(np.eye(16), weak)
    derivs = np.concatenate([tile_weights(along_y), tile_weights(along_z)], axis=1)
    mats = np.concatenate([child_weights(halves), child_weights(projections), derivs], axis=0)
    coefs = np.zeros((32, 128))
    for a in range(4):
        for b in range(4):
            coefs[a * 4 + b, :64] = weak[2 * a, 2 * b]
            coefs[a * 4 + b, 64:] = weak[2 * a + 1, 2 * b + 1]
            coefs[16 + a * 4 + b, :64] = weak[2 * a, 2 * b + 1]
            coefs[16 + a * 4 + b, 64:] = weak[2 * a + 1, 2 * b]

    perm = np.zeros((8, 64), np.int64)
    for code in range(8):
        for s in range(8):
            for t in range(8):
                a, c = (t, s) if code & 4 else (s, t)
                a = 7 - a if code & 1 else a
                c = 7 - c if code & 2 else c
                perm[code, 8 * s + t] = 8 * a + c
    inverse = np.argsort(perm, axis=1)
    lane = np.arange(128)
    rows = []
    for table in (perm, inverse):
        for half in range(2):
            for code in range(8):
                rows.append(table[code][lane % 64] + 64 * half)
    slot_lane = lane % 64
    i, rest = slot_lane // 8, slot_lane % 8
    for end in (7, 0):
        rows.append(64 * (i % 2) + 8 * end + rest)
        rows.append(64 * (i % 2) + 8 * rest + end)
    for kind in range(2):
        for half in range(2):
            for tile in range(4):
                first = 2 * tile + lane // 64
                second = lane % 8 if kind == 0 else (lane // 8) % 8
                rows.append(8 * first + second + 64 * half)
    index = np.repeat(np.stack(rows), 8, axis=0)
    return (
        jnp.asarray(index, i32),
        jnp.asarray(mats, f32).astype(bf16),
        jnp.asarray(coefs, f32),
    )


def take(values, index):
    return jnp.take_along_axis(values, index, axis=1, mode="promise_in_bounds")


def lanes():
    return lax.broadcasted_iota(i32, (8, 128), 1)


def split(values):
    high = values.astype(bf16)
    return high, (values - high.astype(f32)).astype(bf16)


def row(ref, start):
    return ref[pl.ds(pl.multiple_of(start, 8), 8), :]


def child_map(pieces, mats_ref, start, codes):
    high, low = split(jnp.concatenate(pieces, axis=0))
    mapped = jnp.dot(
        jnp.concatenate([high, low, high], axis=1),
        mats_ref[start : start + 384, :],
        preferred_element_type=f32,
    )
    out = []
    for f, piece in enumerate(pieces):
        total = jnp.where(codes == 4, piece, 0.0)
        for c in range(4):
            total = jnp.where(codes == c, mapped[8 * f : 8 * f + 8, 128 * c : 128 * c + 128], total)
        out.append(total)
    return out


def neighbour_part(q, sign, is_z, scale):
    normal = jnp.where(is_z, q[3], q[2]) * sign
    push = q[4] * sign
    return [
        (normal - q[0]) * scale,
        q[1] * -scale,
        (jnp.where(is_z, 0.0, push) - q[2]) * scale,
        (jnp.where(is_z, push, 0.0) - q[3]) * scale,
        (normal - q[4]) * scale,
    ]


def pack_curve(u_ref, slots, masks_ref, index_ref, tmp, left_ref, right_ref):
    low = lanes() < 64
    for side, out_ref, sign in ((0, left_ref, 1.0), (1, right_ref, -1.0)):
        for k in range(8):
            picked = []
            for s in (16 * side + k, 16 * side + k + 8):
                trace = row(u_ref, slots[s] + 768 * side)
                picked.append(take(trace, row(index_ref, slots[64 + s] + INV + 64 * side)))
            tmp[64 * side + 8 * k : 64 * side + 8 * k + 8, :] = jnp.where(low, *picked)
        q = [tmp[pl.ds(64 * side + f, 8, stride=8), :] for f in range(5)]
        scale = masks_ref[CURVE_LIVE + 8 * side : CURVE_LIVE + 8 * side + 8, :] * 14.0
        parts = [
            (sign * q[1] - q[0]) * scale,
            (sign * q[4] - q[1]) * scale,
            q[2] * -scale,
            q[3] * -scale,
            (sign * q[1] - q[4]) * scale,
        ]
        for f in range(5):
            out_ref[pl.ds(f, 8, stride=8), :] = parts[f]


def pack_tile(u_ref, slots, masks_ref, index_ref, mats_ref, tmp, own_ref, tile_ref, ready=None):
    low = lanes() < 64
    quarter = (lanes() % 64) // 16
    for side in range(2):
        for p in range(8):
            picked = []
            for k in range(2):
                s = 32 + 16 * side + 2 * p + k
                index = row(index_ref, slots[128 + s] * 8 + PICK + 16 * side)
                trace = take(row(u_ref, slots[s]), index)
                for a in range(1, 4):
                    other = take(row(u_ref, slots[s] + 256 * a), index)
                    trace = jnp.where(quarter == a, other, trace)
                picked.append(trace)
            pair = jnp.where(low, *picked)
            if side == 1:
                s = 48 + 2 * p
                pair = jnp.where(
                    low,
                    take(pair, row(index_ref, slots[64 + s] + INV)),
                    take(pair, row(index_ref, slots[65 + s] + INV + 64)),
                )
            tmp[64 * side + 8 * p : 64 * side + 8 * p + 8, :] = pair
    q = [tmp[pl.ds(f, 8, stride=8), :] for f in range(5)]
    if ready is not None:
        ready.wait()
    q = child_map(q, mats_ref, 0, masks_ref[CHILD : CHILD + 8, :])
    is_z = masks_ref[SEND_Z : SEND_Z + 8, :] > 0.0
    for f, part in enumerate(neighbour_part(q, -1.0, is_z, 14.0)):
        tile_ref[pl.ds(f, 8, stride=16), :] = part
        own_ref[pl.ds(f, 8, stride=8), :] = part
    q = [tmp[pl.ds(64 + f, 8, stride=8), :] for f in range(5)]
    is_z = masks_ref[RECV_Z : RECV_Z + 8, :] > 0.0
    scale = masks_ref[RECV_LIVE : RECV_LIVE + 8, :] * 14.0
    for f, part in enumerate(neighbour_part(q, 1.0, is_z, scale)):
        tile_ref[pl.ds(8 + f, 8, stride=16), :] = part


def spread(w_refs, pair, slots, s, half, end, index_ref):
    kind = slots[128 + s]
    lane = lanes()
    position = jnp.where(kind == 0, (lane // 8) % 8, lane % 8)
    at_face = position == end
    for a in range(4):
        moved = take(pair, row(index_ref, kind * 64 + SPREAD + 32 * half + 8 * a))
        block = pl.ds(pl.multiple_of(slots[s], 8), 8)
        w_refs[a][block, :] = w_refs[a][block, :] - jnp.where(at_face, moved, 0.0)


def unpack(w_refs, slots, masks_ref, index_ref, mats_ref, tmp, from_left, from_right, tile_ref, own_ref):
    low = lanes() < 64
    q = [
        tile_ref[pl.ds(8 + f, 8, stride=16), :] - own_ref[pl.ds(f, 8, stride=8), :]
        for f in range(5)
    ]
    q = child_map(q, mats_ref, 384, masks_ref[CHILD : CHILD + 8, :])
    for f in range(5):
        tmp[pl.ds(f, 8, stride=8), :] = q[f]
    for side, in_ref in ((0, from_left), (1, from_right)):
        for k in range(8):
            pair = in_ref[8 * k : 8 * k + 8, :]
            turned = pltpu.roll(pair, 64, 1)
            for s, value in ((k, (pair, turned)[side]), (k + 8, (turned, pair)[side])):
                w_ref = w_refs[3 * side]
                block = pl.ds(pl.multiple_of(slots[16 * side + s], 8), 8)
                kept = jnp.where(low, value, 0.0) if side == 0 else jnp.where(low, 0.0, value)
                w_ref[block, :] = w_ref[block, :] - kept
    for p in range(8):
        s = 48 + 2 * p
        pair = tile_ref[16 * p : 16 * p + 8, :]
        pair = jnp.where(
            low,
            take(pair, row(index_ref, slots[64 + s] + PERM)),
            take(pair, row(index_ref, slots[65 + s] + PERM + 64)),
        )
        for k in range(2):
            spread(w_refs, pair, slots, s + k, k, 0, index_ref)
    for p in range(8):
        pair = tmp[8 * p : 8 * p + 8, :]
        for k in range(2):
            spread(w_refs, pair, slots, 32 + 2 * p + k, k, 7, index_ref)


def inside(u_ref, faces_ref, mats_ref, coefs_ref, w_refs):
    fields = [[u_ref[pl.ds(256 * a + f, 32, stride=8), :] for a in range(4)] for f in range(5)]
    dens, vx, vy, vz, pres = fields

    def along(vel, start):
        stacked = [values[a] for values in (vel, pres) for a in range(4)]
        high, low = split(jnp.concatenate(stacked, axis=0))
        both = jnp.dot(
            jnp.concatenate([high, low], axis=1),
            mats_ref[768:1024, start : start + 256],
            preferred_element_type=f32,
        )
        both = both[:, :128] + both[:, 128:]
        return [both[32 * n : 32 * n + 32] for n in range(8)]

    grad_y = along(vy, 0)
    grad_z = along(vz, 256)
    grad_x = []
    for values in (vx, pres):
        plain = values
        turned = [pltpu.roll(t, 64, 1) for t in plain]
        for a in range(4):
            total = None
            for b in range(4):
                n = 4 * a + b
                term = plain[b] * coefs_ref[n : n + 1, :] + turned[b] * coefs_ref[16 + n : 17 + n, :]
                total = term if total is None else total + term
            grad_x.append(total)
    face = [faces_ref[32 * n : 32 * n + 32, :] for n in range(11)]
    ay, az, ayz, ax0, ux0, ax3, ux3, uy0, uy7, uz0, uz7 = face
    for a in range(4):
        d, x, y, z, p = (values[a] for values in fields)
        asum = ayz
        inward = -(ay * y + az * z)
        if a == 0:
            asum = asum + ax0
            inward = inward - ax0 * x
        elif a == 3:
            asum = asum + ax3
            inward = inward + ax3 * x
        diverge = grad_x[a] + grad_y[a] + grad_z[a] - inward
        out = [diverge - asum * d, grad_x[4 + a] - ayz * x, None, None, diverge - asum * p]
        if a == 0:
            out[1] = out[1] + ux0 * (p - x)
        elif a == 3:
            out[1] = out[1] - ux3 * (p + x)
        out[2] = grad_y[4 + a] + uy0 * (p - y) - uy7 * (p + y) - (asum - ay) * y
        out[3] = grad_z[4 + a] + uz0 * (p - z) - uz7 * (p + z) - (asum - az) * z
        for f in range(5):
            w_refs[a][pl.ds(f, 32, stride=8), :] = out[f]


def first_kernel(
    state_hbm, send_faces_hbm, send_counts_hbm, recv_faces_hbm, recv_orients_hbm,
    recv_counts_hbm, curve_faces_hbm, curve_orients_hbm, curve_counts_hbm, index_hbm, mats_hbm, coefs_hbm,
    u_ref, left_ref, right_ref, own_ref, tile_hbm, slots_any, masks_ref, index_ref, mats_ref, coefs_ref,
    send_faces, send_counts, recv_faces, recv_orients, recv_counts, curve_faces,
    curve_orients, curve_counts, slots, state_ref, tmp, tile_ref, sems,
):
    numbers = [
        pltpu.make_async_copy(source, target, sems.at[n])
        for n, (source, target) in enumerate(
            (
                (curve_faces_hbm, curve_faces),
                (curve_orients_hbm, curve_orients),
                (curve_counts_hbm, curve_counts),
                (send_faces_hbm, send_faces),
                (send_counts_hbm, send_counts),
                (recv_faces_hbm, recv_faces),
                (recv_orients_hbm, recv_orients),
                (recv_counts_hbm, recv_counts),
            )
        )
    ]
    arrays = [
        pltpu.make_async_copy(source, target, sems.at[8 + n])
        for n, (source, target) in enumerate(
            (
                (state_hbm, state_ref),
                (index_hbm, index_ref),
                (mats_hbm.at[pl.ds(0, 384), :], mats_ref.at[pl.ds(0, 384), :]),
                (mats_hbm.at[pl.ds(384, 640), :], mats_ref.at[pl.ds(384, 640), :]),
                (coefs_hbm, coefs_ref),
            )
        )
    ]
    for copy in numbers + arrays:
        copy.start()
    for copy in numbers:
        copy.wait()
    low = lax.broadcasted_iota(i32, (1, 128), 1) < 64

    def halves(a, b):
        return jnp.where(low, a, b)

    for side in range(2):
        live = []
        for k in range(16):
            s = 16 * side + k
            is_live = k < curve_counts[side]
            element = (curve_faces[side, k] * 10923) >> 16
            slots[s] = element * 8
            slots[64 + s] = curve_orients[side, k] * 8
            live.append(jnp.where(is_live, 1.0, 0.0))
        for k in range(8):
            at = CURVE_LIVE + 8 * side + k
            masks_ref[at : at + 1, :] = halves(live[k], live[k + 8])
    for p in range(8):
        child, kinds, recv_kinds, recv_live = [], [], [], []
        for k in range(2):
            s = 32 + 2 * p + k
            number = send_faces[k, p]
            is_live = k < send_counts[p]
            element = (number * 2185) >> 16
            rest = number - 30 * element
            is_z = rest >= 25
            slots[s] = element * 8
            slots[128 + s] = jnp.where(is_z, 1, 0)
            child.append(jnp.where(is_live, jnp.where(is_z, rest - 25, rest - 15), -1))
            kinds.append(jnp.where(is_z, 1.0, 0.0))
            s = 48 + 2 * p + k
            number = recv_faces[k, p]
            is_live = k < recv_counts[p]
            element = (number * 10923) >> 16
            is_z = number - 6 * element == 4
            slots[s] = element * 8
            slots[64 + s] = recv_orients[k, p] * 8
            slots[128 + s] = jnp.where(is_z, 1, 0)
            recv_kinds.append(jnp.where(is_z, 1.0, 0.0))
            recv_live.append(jnp.where(is_live, 1.0, 0.0))
        masks_ref[CHILD + p : CHILD + p + 1, :] = halves(*child).astype(f32)
        masks_ref[SEND_Z + p : SEND_Z + p + 1, :] = halves(*kinds)
        masks_ref[RECV_Z + p : RECV_Z + p + 1, :] = halves(*recv_kinds)
        masks_ref[RECV_LIVE + p : RECV_LIVE + p + 1, :] = halves(*recv_live)
    keep = pltpu.make_async_copy(slots, slots_any, sems.at[13])
    keep.start()
    arrays[0].wait()
    for f in range(5):
        for a in range(4):
            u_ref[pl.ds(256 * a + f, 32, stride=8), :] = state_ref[f, :, 128 * a : 128 * a + 128]
    arrays[1].wait()
    pack_tile(
        u_ref, slots, masks_ref, index_ref, mats_ref, tmp, own_ref, tile_ref, ready=arrays[2]
    )
    send = pltpu.make_async_copy(tile_ref, tile_hbm, sems.at[14])
    send.start()
    pack_curve(u_ref, slots, masks_ref, index_ref, tmp, left_ref, right_ref)
    for copy in (*arrays[3:], keep, send):
        copy.wait()


def faces_kernel(
    slots, levels, send_counts, recv_counts, curve_counts, faces_ref, scale_ref, listed
):
    listed[...] = jnp.zeros_like(listed)
    for s in range(64):
        element = slots[s] >> 3
        if s < 32:
            is_live = s % 16 < curve_counts[s // 16]
            at = 32 * (s // 16) + element
        elif s < 48:
            is_live = s % 2 < send_counts[s % 16 // 2]
            at = 96 + 64 * slots[128 + s] + element
        else:
            is_live = s % 2 < recv_counts[s % 16 // 2]
            at = 64 + 64 * slots[128 + s] + element
        listed[pl.ds(jnp.where(is_live, at, 192), 1), :] = jnp.ones((1, 128), f32)
    for e in range(32):
        scale_ref[8 * e : 8 * e + 8, :] = (
            jnp.full((8, 128), 1 << levels[e], i32).astype(f32) * time_step
        )
    lane = lax.broadcasted_iota(i32, (32, 128), 1)
    on = [listed[32 * f : 32 * f + 32, :] for f in range(6)]
    where_0 = [lane < 64, (lane // 8) % 8 == 0, lane % 8 == 0]
    where_7 = [lane >= 64, (lane // 8) % 8 == 7, lane % 8 == 7]

    def keep(test, values):
        return jnp.where(test, values, 0.0)

    ay = keep(where_0[1], 14.0 * on[2])
    az = keep(where_0[2], 14.0 * on[4])
    values = [
        ay,
        az,
        ay + az,
        keep(where_0[0], 14.0 * on[0]),
        keep(where_0[0], 28.0 - 14.0 * on[0]),
        keep(where_7[0], 14.0 * on[1]),
        keep(where_7[0], 28.0 - 14.0 * on[1]),
        keep(where_0[1], 28.0 - 14.0 * on[2]),
        keep(where_7[1], 28.0 - 28.0 * on[3]),
        keep(where_0[2], 28.0 - 14.0 * on[4]),
        keep(where_7[2], 28.0 - 28.0 * on[5]),
    ]
    for n, value in enumerate(values):
        faces_ref[32 * n : 32 * n + 32, :] = value


def next_kernel(
    slots_any, u_ref, from_left, from_right, arrived_ref, sent_ref, masks_ref, faces_ref, scale_ref,
    index_ref, mats_ref, coefs_ref,
    out_ref, left_ref, right_ref, own_ref, tile_hbm, w_0, w_1, w_2, w_3, tmp, slots, tile_ref, sems,
):
    w_refs = (w_0, w_1, w_2, w_3)
    fetch = pltpu.make_async_copy(slots_any, slots, sems.at[0])
    fetch.start()
    inside(u_ref, faces_ref, mats_ref, coefs_ref, w_refs)
    fetch.wait()
    unpack(
        w_refs, slots, masks_ref, index_ref, mats_ref, tmp, from_left, from_right, arrived_ref, sent_ref
    )
    for a in range(4):
        out_ref[256 * a : 256 * a + 256, :] = w_refs[a][...] * scale_ref[...]
    pack_tile(out_ref, slots, masks_ref, index_ref, mats_ref, tmp, own_ref, tile_ref)
    send = pltpu.make_async_copy(tile_ref, tile_hbm, sems.at[1])
    send.start()
    pack_curve(out_ref, slots, masks_ref, index_ref, tmp, left_ref, right_ref)
    send.wait()


def last_kernel(
    slots_any, u_ref, from_left, from_right, arrived_ref, sent_ref, masks_ref, faces_ref, scale_ref,
    index_ref, mats_ref, coefs_ref, state_ref, first_ref,
    out_ref, w_0, w_1, w_2, w_3, tmp, slots, sems,
):
    w_refs = (w_0, w_1, w_2, w_3)
    fetch = pltpu.make_async_copy(slots_any, slots, sems.at[0])
    fetch.start()
    inside(u_ref, faces_ref, mats_ref, coefs_ref, w_refs)
    fetch.wait()
    unpack(
        w_refs, slots, masks_ref, index_ref, mats_ref, tmp, from_left, from_right, arrived_ref, sent_ref
    )
    scale = scale_ref[pl.ds(0, 32, stride=8), :] * (1.0 / 6.0)
    for f in range(5):
        for a in range(4):
            at = (pl.ds(256 * a + f, 32, stride=8), slice(None))
            column = slice(128 * a, 128 * a + 128)
            out_ref[f, :, column] = (
                state_ref[f, :, column]
                + first_ref[at]
                + 0.5 * u_ref[at]
                + w_refs[a][pl.ds(f, 32, stride=8), :] * scale
            )


def shards(
    state, levels, send_faces, send_counts, recv_faces, recv_orients, recv_counts,
    curve_faces, curve_orients, curve_counts,
):
    index, mats, coefs = tables()
    vmem = pl.BlockSpec(memory_space=pltpu.VMEM)
    smem = pl.BlockSpec(memory_space=pltpu.SMEM)
    hbm = pl.BlockSpec(memory_space=pltpu.HBM)
    anywhere = pl.BlockSpec(memory_space=pl.ANY)

    def shape(*dims, kind=f32):
        return jax.ShapeDtypeStruct(dims, kind)

    def call(kernel, name, **kwargs):
        return pl.pallas_call(
            kernel,
            name=name,
            compiler_params=pltpu.CompilerParams(vmem_limit_bytes=16 * 1024 * 1024),
            **kwargs,
        )

    payload = [shape(64, 128)] * 3 + [shape(128, 128)]
    n_curve = lax.axis_size("curve")
    rightward = [(i, i + 1) for i in range(n_curve - 1)]
    leftward = [(i + 1, i) for i in range(n_curve - 1)]

    def exchange(left, right, tile):
        arrived = lax.all_to_all(
            tile.reshape(8, 16, 128), "tile", split_axis=0, concat_axis=0, tiled=True
        )
        from_left = lax.ppermute(right, "curve", rightward)
        from_right = lax.ppermute(left, "curve", leftward)
        return from_left, from_right, arrived.reshape(128, 128)

    numbers = [
        send_faces.T, send_counts, recv_faces.T, recv_orients.T, recv_counts,
        curve_faces, curve_orients, curve_counts,
    ]
    u, left, right, own, tile, slots, masks, index, mats, coefs = call(
        first_kernel,
        "first",
        out_shape=[shape(1024, 128), *payload, shape(256, kind=i32), shape(48, 128)]
        + [shape(*x.shape, kind=x.dtype) for x in (index, mats, coefs)],
        in_specs=[hbm] * 12,
        out_specs=[vmem] * 4 + [hbm, anywhere] + [vmem] * 4,
        scratch_shapes=[pltpu.SMEM(x.shape, i32) for x in numbers] + [pltpu.SMEM((256,), i32)]
        + [
            pltpu.VMEM(state.shape, f32),
            pltpu.VMEM((128, 128), f32),
            pltpu.VMEM((128, 128), f32),
            pltpu.SemaphoreType.DMA((15,)),
        ],
    )(*[pltpu.with_memory_space_constraint(x, pltpu.HBM) for x in (state, *numbers, index, mats, coefs)])
    scratch = [pltpu.VMEM((256, 128), f32)] * 4
    scratch += [pltpu.VMEM((128, 128), f32), pltpu.SMEM((256,), i32)]
    sems = pltpu.SemaphoreType.DMA((2,))
    kept = []
    for section in range(3):
        from_left, from_right, arrived = exchange(left, right, tile)
        if section == 0:
            faces, scale = call(
                faces_kernel,
                "faces",
                out_shape=[shape(352, 128), shape(256, 128)],
                in_specs=[smem] * 5,
                out_specs=[vmem] * 2,
                scratch_shapes=[pltpu.VMEM((200, 128), f32)],
                cost_estimate=pl.CostEstimate(
                    flops=20_000_000, bytes_accessed=1_000_000, transcendentals=0
                ),
            )(slots, levels, send_counts, recv_counts, curve_counts)
        args = (
            slots, u, from_left, from_right, arrived, own, masks, faces, scale,
            index, mats, coefs,
        )
        if section < 2:
            u, left, right, own, tile = call(
                next_kernel,
                "next",
                out_shape=[shape(1024, 128), *payload],
                in_specs=[anywhere] + [vmem] * 11,
                out_specs=[vmem] * 4 + [hbm],
                scratch_shapes=[*scratch, pltpu.VMEM((128, 128), f32), sems],
            )(*args)
            kept.append(u)
    return call(
        last_kernel,
        "last",
        out_shape=shape(5, 32, 512),
        in_specs=[anywhere] + [vmem] * 13,
        out_specs=vmem,
        scratch_shapes=[*scratch, sems],
    )(*args, state, kept[0])


def solution(mesh):
    both = P(("curve", "tile"))
    rows = P(("curve", "tile"), None)
    return jax.shard_map(
        shards,
        mesh=mesh,
        in_specs=(P(None, ("curve", "tile"), None), both, rows, both, rows, rows, both, rows, rows, both),
        out_specs=P(None, ("curve", "tile"), None),
        check_vma=False,
    )
```

```python
import jax
import jax.numpy as jnp
import numpy as np
from jax import lax
from jax.experimental import pallas as pl
from jax.experimental.pallas import tpu as pltpu
from jax.sharding import PartitionSpec as P


time_step = 0.002
inner_nodes = [
    -0.8717401485096066,
    -0.5917001814331423,
    -0.20929921790247888,
    0.20929921790247888,
    0.5917001814331423,
    0.8717401485096066,
]
f32, bf16, i32 = jnp.float32, jnp.bfloat16, jnp.int32

PERM, INV, PICK, SPREAD, INDEX_ROWS = 0, 128, 256, 288, 416
CHILD, SEND_Z, RECV_Z, RECV_LIVE, CURVE_LIVE = 0, 8, 16, 24, 32


def legendre_seven(abscissa):
    before = abscissa * 0.0 + 1.0
    current = abscissa + 0.0
    for order in range(1, 7):
        before, current = (
            current,
            ((2 * order + 1) * abscissa * current - order * before) / (order + 1),
        )
    return current


def split_np(array):
    array = np.asarray(array, np.float32).astype(np.float64)
    high = array.astype(bf16).astype(np.float64)
    low = (array - high).astype(bf16).astype(np.float64)
    return high, low


def tables():
    degree = 7
    points = np.array([-1.0] + inner_nodes + [1.0])
    values = legendre_seven(points)
    weights = 2.0 / (degree * (degree + 1) * values**2)
    deriv = np.zeros((8, 8))
    for i in range(8):
        for m in range(8):
            if i != m:
                deriv[i, m] = values[i] / (values[m] * (points[i] - points[m]))
    deriv[0, 0] = -degree * (degree + 1) / 4.0
    deriv[7, 7] = degree * (degree + 1) / 4.0
    weak = -deriv
    weak[0, 0] -= 28.0
    weak[7, 7] += 28.0
    halves, projections = [], []
    for side in range(2):
        targets = (points + 2.0 * side - 1.0) / 2.0
        interp = np.ones((8, 8))
        for m in range(8):
            for other in range(8):
                if other != m:
                    interp[:, m] *= (targets - points[other]) / (points[m] - points[other])
        halves.append(interp)
        projections.append(0.5 * (interp.T * weights[None, :]) / weights[:, None])

    def child_weights(parts):
        columns = [
            np.kron(np.eye(2), np.kron(parts[a], parts[b]).T) for a in range(2) for b in range(2)
        ]
        high, low = split_np(np.concatenate(columns, axis=1))
        return np.concatenate([high, high, low], axis=0)

    def tile_weights(matrix):
        high, low = split_np(matrix.T)
        return np.block([[high, low], [high, np.zeros_like(high)]])

    along_y = np.kron(np.eye(2), np.kron(weak, np.eye(8)))
    along_z = np.kron(np.eye(16), weak)
    derivs = np.concatenate([tile_weights(along_y), tile_weights(along_z)], axis=1)
    mats = np.concatenate([child_weights(halves), child_weights(projections), derivs], axis=0)
    coefs = np.zeros((32, 128))
    for a in range(4):
        for b in range(4):
            coefs[a * 4 + b, :64] = weak[2 * a, 2 * b]
            coefs[a * 4 + b, 64:] = weak[2 * a + 1, 2 * b + 1]
            coefs[16 + a * 4 + b, :64] = weak[2 * a, 2 * b + 1]
            coefs[16 + a * 4 + b, 64:] = weak[2 * a + 1, 2 * b]

    perm = np.zeros((8, 64), np.int64)
    for code in range(8):
        for s in range(8):
            for t in range(8):
                a, c = (t, s) if code & 4 else (s, t)
                a = 7 - a if code & 1 else a
                c = 7 - c if code & 2 else c
                perm[code, 8 * s + t] = 8 * a + c
    inverse = np.argsort(perm, axis=1)
    lane = np.arange(128)
    rows = []
    for table in (perm, inverse):
        for half in range(2):
            for code in range(8):
                rows.append(table[code][lane % 64] + 64 * half)
    slot_lane = lane % 64
    i, rest = slot_lane // 8, slot_lane % 8
    for end in (7, 0):
        rows.append(64 * (i % 2) + 8 * end + rest)
        rows.append(64 * (i % 2) + 8 * rest + end)
    for kind in range(2):
        for half in range(2):
            for tile in range(4):
                first = 2 * tile + lane // 64
                second = lane % 8 if kind == 0 else (lane // 8) % 8
                rows.append(8 * first + second + 64 * half)
    index = np.repeat(np.stack(rows), 8, axis=0)
    return (
        jnp.asarray(index, i32),
        jnp.asarray(mats, f32).astype(bf16),
        jnp.asarray(coefs, f32),
    )


def take(values, index):
    return jnp.take_along_axis(values, index, axis=1, mode="promise_in_bounds")


def lanes():
    return lax.broadcasted_iota(i32, (8, 128), 1)


def split(values):
    high = values.astype(bf16)
    return high, (values - high.astype(f32)).astype(bf16)


def row(ref, start):
    return ref[pl.ds(pl.multiple_of(start, 8), 8), :]


def child_map(pieces, mats_ref, start, codes):
    high, low = split(jnp.concatenate(pieces, axis=0))
    mapped = jnp.dot(
        jnp.concatenate([high, low, high], axis=1),
        mats_ref[start : start + 384, :],
        preferred_element_type=f32,
    )
    out = []
    for f, piece in enumerate(pieces):
        total = jnp.where(codes == 4, piece, 0.0)
        for c in range(4):
            total = jnp.where(codes == c, mapped[8 * f : 8 * f + 8, 128 * c : 128 * c + 128], total)
        out.append(total)
    return out


def neighbour_part(q, sign, is_z, scale):
    normal = jnp.where(is_z, q[3], q[2]) * sign
    push = q[4] * sign
    return [
        (normal - q[0]) * scale,
        q[1] * -scale,
        (jnp.where(is_z, 0.0, push) - q[2]) * scale,
        (jnp.where(is_z, push, 0.0) - q[3]) * scale,
        (normal - q[4]) * scale,
    ]


def pack_curve(u_ref, slots, masks_ref, index_ref, tmp, left_ref, right_ref):
    low = lanes() < 64
    for side, out_ref, sign in ((0, left_ref, 1.0), (1, right_ref, -1.0)):
        for k in range(8):
            picked = []
            for s in (16 * side + k, 16 * side + k + 8):
                trace = row(u_ref, slots[s] + 768 * side)
                picked.append(take(trace, row(index_ref, slots[64 + s] + INV + 64 * side)))
            tmp[64 * side + 8 * k : 64 * side + 8 * k + 8, :] = jnp.where(low, *picked)
        q = [tmp[pl.ds(64 * side + f, 8, stride=8), :] for f in range(5)]
        scale = masks_ref[CURVE_LIVE + 8 * side : CURVE_LIVE + 8 * side + 8, :] * 14.0
        parts = [
            (sign * q[1] - q[0]) * scale,
            (sign * q[4] - q[1]) * scale,
            q[2] * -scale,
            q[3] * -scale,
            (sign * q[1] - q[4]) * scale,
        ]
        for f in range(5):
            out_ref[8 * f : 8 * f + 8, :] = parts[f]


def pack_tile(u_ref, slots, masks_ref, index_ref, mats_ref, tmp, own_ref, tile_ref, ready=None):
    low = lanes() < 64
    quarter = (lanes() % 64) // 16
    for side in range(2):
        for p in range(8):
            picked = []
            for k in range(2):
                s = 32 + 16 * side + 2 * p + k
                index = row(index_ref, slots[128 + s] * 8 + PICK + 16 * side)
                trace = take(row(u_ref, slots[s]), index)
                for a in range(1, 4):
                    other = take(row(u_ref, slots[s] + 256 * a), index)
                    trace = jnp.where(quarter == a, other, trace)
                picked.append(trace)
            pair = jnp.where(low, *picked)
            if side == 1:
                s = 48 + 2 * p
                pair = jnp.where(
                    low,
                    take(pair, row(index_ref, slots[64 + s] + INV)),
                    take(pair, row(index_ref, slots[65 + s] + INV + 64)),
                )
            tmp[64 * side + 8 * p : 64 * side + 8 * p + 8, :] = pair
    q = [tmp[pl.ds(f, 8, stride=8), :] for f in range(5)]
    if ready is not None:
        ready.wait()
    q = child_map(q, mats_ref, 0, masks_ref[CHILD : CHILD + 8, :])
    is_z = masks_ref[SEND_Z : SEND_Z + 8, :] > 0.0
    for f, part in enumerate(neighbour_part(q, -1.0, is_z, 14.0)):
        tile_ref[pl.ds(f, 8, stride=16), :] = part
        own_ref[pl.ds(f, 8, stride=8), :] = part
    q = [tmp[pl.ds(64 + f, 8, stride=8), :] for f in range(5)]
    is_z = masks_ref[RECV_Z : RECV_Z + 8, :] > 0.0
    scale = masks_ref[RECV_LIVE : RECV_LIVE + 8, :] * 14.0
    for f, part in enumerate(neighbour_part(q, 1.0, is_z, scale)):
        tile_ref[pl.ds(8 + f, 8, stride=16), :] = part


def spread(w_refs, pair, slots, s, half, end, index_ref):
    kind = slots[128 + s]
    lane = lanes()
    position = jnp.where(kind == 0, (lane // 8) % 8, lane % 8)
    at_face = position == end
    for a in range(4):
        moved = take(pair, row(index_ref, kind * 64 + SPREAD + 32 * half + 8 * a))
        block = pl.ds(pl.multiple_of(slots[s], 8), 8)
        w_refs[a][block, :] = w_refs[a][block, :] - jnp.where(at_face, moved, 0.0)


def unpack(w_refs, slots, masks_ref, index_ref, mats_ref, tmp, from_left, from_right, tile_ref, own_ref):
    low = lanes() < 64
    q = [
        tile_ref[pl.ds(8 + f, 8, stride=16), :] - own_ref[pl.ds(f, 8, stride=8), :]
        for f in range(5)
    ]
    q = child_map(q, mats_ref, 384, masks_ref[CHILD : CHILD + 8, :])
    for f in range(5):
        tmp[pl.ds(f, 8, stride=8), :] = q[f]
    for side, in_ref in ((0, from_left), (1, from_right)):
        for f in range(5):
            tmp[pl.ds(64 + 64 * side + f, 8, stride=8), :] = in_ref[8 * f : 8 * f + 8, :]
        for k in range(8):
            pair = tmp[64 + 64 * side + 8 * k : 72 + 64 * side + 8 * k, :]
            turned = pltpu.roll(pair, 64, 1)
            for s, value in ((k, (pair, turned)[side]), (k + 8, (turned, pair)[side])):
                w_ref = w_refs[3 * side]
                block = pl.ds(pl.multiple_of(slots[16 * side + s], 8), 8)
                kept = jnp.where(low, value, 0.0) if side == 0 else jnp.where(low, 0.0, value)
                w_ref[block, :] = w_ref[block, :] - kept
    for p in range(8):
        s = 48 + 2 * p
        pair = tile_ref[16 * p : 16 * p + 8, :]
        pair = jnp.where(
            low,
            take(pair, row(index_ref, slots[64 + s] + PERM)),
            take(pair, row(index_ref, slots[65 + s] + PERM + 64)),
        )
        for k in range(2):
            spread(w_refs, pair, slots, s + k, k, 0, index_ref)
    for p in range(8):
        pair = tmp[8 * p : 8 * p + 8, :]
        for k in range(2):
            spread(w_refs, pair, slots, 32 + 2 * p + k, k, 7, index_ref)


def inside(u_ref, faces_ref, mats_ref, coefs_ref, w_refs):
    fields = [[u_ref[pl.ds(256 * a + f, 32, stride=8), :] for a in range(4)] for f in range(5)]
    dens, vx, vy, vz, pres = fields

    def along(vel, start):
        stacked = [values[a] for values in (vel, pres) for a in range(4)]
        high, low = split(jnp.concatenate(stacked, axis=0))
        both = jnp.dot(
            jnp.concatenate([high, low], axis=1),
            mats_ref[768:1024, start : start + 256],
            preferred_element_type=f32,
        )
        both = both[:, :128] + both[:, 128:]
        return [both[32 * n : 32 * n + 32] for n in range(8)]

    grad_y = along(vy, 0)
    grad_z = along(vz, 256)
    grad_x = []
    for values in (vx, pres):
        plain = values
        turned = [pltpu.roll(t, 64, 1) for t in plain]
        for a in range(4):
            total = None
            for b in range(4):
                n = 4 * a + b
                term = plain[b] * coefs_ref[n : n + 1, :] + turned[b] * coefs_ref[16 + n : 17 + n, :]
                total = term if total is None else total + term
            grad_x.append(total)
    face = [faces_ref[32 * n : 32 * n + 32, :] for n in range(11)]
    ay, az, ayz, ax0, ux0, ax3, ux3, uy0, uy7, uz0, uz7 = face
    for a in range(4):
        d, x, y, z, p = (values[a] for values in fields)
        asum = ayz
        inward = -(ay * y + az * z)
        if a == 0:
            asum = asum + ax0
            inward = inward - ax0 * x
        elif a == 3:
            asum = asum + ax3
            inward = inward + ax3 * x
        diverge = grad_x[a] + grad_y[a] + grad_z[a] - inward
        out = [diverge - asum * d, grad_x[4 + a] - ayz * x, None, None, diverge - asum * p]
        if a == 0:
            out[1] = out[1] + ux0 * (p - x)
        elif a == 3:
            out[1] = out[1] - ux3 * (p + x)
        out[2] = grad_y[4 + a] + uy0 * (p - y) - uy7 * (p + y) - (asum - ay) * y
        out[3] = grad_z[4 + a] + uz0 * (p - z) - uz7 * (p + z) - (asum - az) * z
        for f in range(5):
            w_refs[a][pl.ds(f, 32, stride=8), :] = out[f]


def first_kernel(
    state_hbm, send_faces_hbm, send_counts_hbm, recv_faces_hbm, recv_orients_hbm,
    recv_counts_hbm, curve_faces_hbm, curve_orients_hbm, curve_counts_hbm, index_hbm, mats_hbm, coefs_hbm,
    u_ref, left_ref, right_ref, own_ref, tile_hbm, slots_any, masks_ref, index_ref, mats_ref, coefs_ref,
    send_faces, send_counts, recv_faces, recv_orients, recv_counts, curve_faces,
    curve_orients, curve_counts, slots, state_ref, tmp, tile_ref, sems,
):
    numbers = [
        pltpu.make_async_copy(source, target, sems.at[n])
        for n, (source, target) in enumerate(
            (
                (curve_faces_hbm, curve_faces),
                (curve_orients_hbm, curve_orients),
                (curve_counts_hbm, curve_counts),
                (send_faces_hbm, send_faces),
                (send_counts_hbm, send_counts),
                (recv_faces_hbm, recv_faces),
                (recv_orients_hbm, recv_orients),
                (recv_counts_hbm, recv_counts),
            )
        )
    ]
    arrays = [
        pltpu.make_async_copy(source, target, sems.at[8 + n])
        for n, (source, target) in enumerate(
            (
                (state_hbm, state_ref),
                (index_hbm, index_ref),
                (mats_hbm.at[pl.ds(0, 384), :], mats_ref.at[pl.ds(0, 384), :]),
                (mats_hbm.at[pl.ds(384, 640), :], mats_ref.at[pl.ds(384, 640), :]),
                (coefs_hbm, coefs_ref),
            )
        )
    ]
    for copy in numbers + arrays:
        copy.start()
    for copy in numbers:
        copy.wait()
    low = lax.broadcasted_iota(i32, (1, 128), 1) < 64

    def halves(a, b):
        return jnp.where(low, a, b)

    for side in range(2):
        live = []
        for k in range(16):
            s = 16 * side + k
            is_live = k < curve_counts[side]
            element = (curve_faces[side, k] * 10923) >> 16
            slots[s] = element * 8
            slots[64 + s] = curve_orients[side, k] * 8
            live.append(jnp.where(is_live, 1.0, 0.0))
        for k in range(8):
            at = CURVE_LIVE + 8 * side + k
            masks_ref[at : at + 1, :] = halves(live[k], live[k + 8])
    for p in range(8):
        child, kinds, recv_kinds, recv_live = [], [], [], []
        for k in range(2):
            s = 32 + 2 * p + k
            number = send_faces[k, p]
            is_live = k < send_counts[p]
            element = (number * 2185) >> 16
            rest = number - 30 * element
            is_z = rest >= 25
            slots[s] = element * 8
            slots[128 + s] = jnp.where(is_z, 1, 0)
            child.append(jnp.where(is_live, jnp.where(is_z, rest - 25, rest - 15), -1))
            kinds.append(jnp.where(is_z, 1.0, 0.0))
            s = 48 + 2 * p + k
            number = recv_faces[k, p]
            is_live = k < recv_counts[p]
            element = (number * 10923) >> 16
            is_z = number - 6 * element == 4
            slots[s] = element * 8
            slots[64 + s] = recv_orients[k, p] * 8
            slots[128 + s] = jnp.where(is_z, 1, 0)
            recv_kinds.append(jnp.where(is_z, 1.0, 0.0))
            recv_live.append(jnp.where(is_live, 1.0, 0.0))
        masks_ref[CHILD + p : CHILD + p + 1, :] = halves(*child).astype(f32)
        masks_ref[SEND_Z + p : SEND_Z + p + 1, :] = halves(*kinds)
        masks_ref[RECV_Z + p : RECV_Z + p + 1, :] = halves(*recv_kinds)
        masks_ref[RECV_LIVE + p : RECV_LIVE + p + 1, :] = halves(*recv_live)
    keep = pltpu.make_async_copy(slots, slots_any, sems.at[13])
    keep.start()
    arrays[0].wait()
    for f in range(5):
        for a in range(4):
            u_ref[pl.ds(256 * a + f, 32, stride=8), :] = state_ref[f, :, 128 * a : 128 * a + 128]
    arrays[1].wait()
    pack_tile(
        u_ref, slots, masks_ref, index_ref, mats_ref, tmp, own_ref, tile_ref, ready=arrays[2]
    )
    send = pltpu.make_async_copy(tile_ref, tile_hbm, sems.at[14])
    send.start()
    pack_curve(u_ref, slots, masks_ref, index_ref, tmp, left_ref, right_ref)
    for copy in (*arrays[3:], keep, send):
        copy.wait()


def faces_kernel(
    slots, levels, send_counts, recv_counts, curve_counts, faces_ref, scale_ref, listed
):
    listed[...] = jnp.zeros_like(listed)
    for s in range(64):
        element = slots[s] >> 3
        if s < 32:
            is_live = s % 16 < curve_counts[s // 16]
            at = 32 * (s // 16) + element
        elif s < 48:
            is_live = s % 2 < send_counts[s % 16 // 2]
            at = 96 + 64 * slots[128 + s] + element
        else:
            is_live = s % 2 < recv_counts[s % 16 // 2]
            at = 64 + 64 * slots[128 + s] + element
        listed[pl.ds(jnp.where(is_live, at, 192), 1), :] = jnp.ones((1, 128), f32)
    for e in range(32):
        scale_ref[8 * e : 8 * e + 8, :] = (
            jnp.full((8, 128), 1 << levels[e], i32).astype(f32) * time_step
        )
    lane = lax.broadcasted_iota(i32, (32, 128), 1)
    on = [listed[32 * f : 32 * f + 32, :] for f in range(6)]
    where_0 = [lane < 64, (lane // 8) % 8 == 0, lane % 8 == 0]
    where_7 = [lane >= 64, (lane // 8) % 8 == 7, lane % 8 == 7]

    def keep(test, values):
        return jnp.where(test, values, 0.0)

    ay = keep(where_0[1], 14.0 * on[2])
    az = keep(where_0[2], 14.0 * on[4])
    values = [
        ay,
        az,
        ay + az,
        keep(where_0[0], 14.0 * on[0]),
        keep(where_0[0], 28.0 - 14.0 * on[0]),
        keep(where_7[0], 14.0 * on[1]),
        keep(where_7[0], 28.0 - 14.0 * on[1]),
        keep(where_0[1], 28.0 - 14.0 * on[2]),
        keep(where_7[1], 28.0 - 28.0 * on[3]),
        keep(where_0[2], 28.0 - 14.0 * on[4]),
        keep(where_7[2], 28.0 - 28.0 * on[5]),
    ]
    for n, value in enumerate(values):
        faces_ref[32 * n : 32 * n + 32, :] = value


def next_kernel(
    slots_any, u_ref, from_left, from_right, arrived_ref, sent_ref, masks_ref, faces_ref, scale_ref,
    index_ref, mats_ref, coefs_ref,
    out_ref, left_ref, right_ref, own_ref, tile_hbm, w_0, w_1, w_2, w_3, tmp, slots, tile_ref, sems,
):
    w_refs = (w_0, w_1, w_2, w_3)
    fetch = pltpu.make_async_copy(slots_any, slots, sems.at[0])
    fetch.start()
    inside(u_ref, faces_ref, mats_ref, coefs_ref, w_refs)
    fetch.wait()
    unpack(
        w_refs, slots, masks_ref, index_ref, mats_ref, tmp, from_left, from_right, arrived_ref, sent_ref
    )
    for a in range(4):
        out_ref[256 * a : 256 * a + 256, :] = w_refs[a][...] * scale_ref[...]
    pack_tile(out_ref, slots, masks_ref, index_ref, mats_ref, tmp, own_ref, tile_ref)
    send = pltpu.make_async_copy(tile_ref, tile_hbm, sems.at[1])
    send.start()
    pack_curve(out_ref, slots, masks_ref, index_ref, tmp, left_ref, right_ref)
    send.wait()


def last_kernel(
    slots_any, u_ref, from_left, from_right, arrived_ref, sent_ref, masks_ref, faces_ref, scale_ref,
    index_ref, mats_ref, coefs_ref, state_ref, first_ref,
    out_ref, w_0, w_1, w_2, w_3, tmp, slots, sems,
):
    w_refs = (w_0, w_1, w_2, w_3)
    fetch = pltpu.make_async_copy(slots_any, slots, sems.at[0])
    fetch.start()
    inside(u_ref, faces_ref, mats_ref, coefs_ref, w_refs)
    fetch.wait()
    unpack(
        w_refs, slots, masks_ref, index_ref, mats_ref, tmp, from_left, from_right, arrived_ref, sent_ref
    )
    scale = scale_ref[pl.ds(0, 32, stride=8), :] * (1.0 / 6.0)
    for f in range(5):
        for a in range(4):
            at = (pl.ds(256 * a + f, 32, stride=8), slice(None))
            column = slice(128 * a, 128 * a + 128)
            out_ref[f, :, column] = (
                state_ref[f, :, column]
                + first_ref[at]
                + 0.5 * u_ref[at]
                + w_refs[a][pl.ds(f, 32, stride=8), :] * scale
            )


def shards(
    state, levels, send_faces, send_counts, recv_faces, recv_orients, recv_counts,
    curve_faces, curve_orients, curve_counts,
):
    index, mats, coefs = tables()
    vmem = pl.BlockSpec(memory_space=pltpu.VMEM)
    smem = pl.BlockSpec(memory_space=pltpu.SMEM)
    hbm = pl.BlockSpec(memory_space=pltpu.HBM)
    anywhere = pl.BlockSpec(memory_space=pl.ANY)

    def shape(*dims, kind=f32):
        return jax.ShapeDtypeStruct(dims, kind)

    def call(kernel, name, **kwargs):
        return pl.pallas_call(
            kernel,
            name=name,
            compiler_params=pltpu.CompilerParams(vmem_limit_bytes=16 * 1024 * 1024),
            **kwargs,
        )

    payload = [shape(40, 128)] * 2 + [shape(64, 128), shape(128, 128)]
    n_curve = lax.axis_size("curve")
    rightward = [(i, i + 1) for i in range(n_curve - 1)]
    leftward = [(i + 1, i) for i in range(n_curve - 1)]

    def exchange(left, right, tile):
        arrived = lax.all_to_all(
            tile.reshape(8, 16, 128), "tile", split_axis=0, concat_axis=0, tiled=True
        )
        from_left = lax.ppermute(right, "curve", rightward)
        from_right = lax.ppermute(left, "curve", leftward)
        return from_left, from_right, arrived.reshape(128, 128)

    numbers = [
        send_faces.T, send_counts, recv_faces.T, recv_orients.T, recv_counts,
        curve_faces, curve_orients, curve_counts,
    ]
    u, left, right, own, tile, slots, masks, index, mats, coefs = call(
        first_kernel,
        "first",
        out_shape=[shape(1024, 128), *payload, shape(256, kind=i32), shape(48, 128)]
        + [shape(*x.shape, kind=x.dtype) for x in (index, mats, coefs)],
        in_specs=[hbm] * 12,
        out_specs=[vmem] * 4 + [hbm, anywhere] + [vmem] * 4,
        scratch_shapes=[pltpu.SMEM(x.shape, i32) for x in numbers] + [pltpu.SMEM((256,), i32)]
        + [
            pltpu.VMEM(state.shape, f32),
            pltpu.VMEM((128, 128), f32),
            pltpu.VMEM((128, 128), f32),
            pltpu.SemaphoreType.DMA((15,)),
        ],
    )(*[pltpu.with_memory_space_constraint(x, pltpu.HBM) for x in (state, *numbers, index, mats, coefs)])
    scratch = [pltpu.VMEM((256, 128), f32)] * 4
    scratch += [pltpu.VMEM((192, 128), f32), pltpu.SMEM((256,), i32)]
    sems = pltpu.SemaphoreType.DMA((2,))
    kept = []
    for section in range(3):
        from_left, from_right, arrived = exchange(left, right, tile)
        if section == 0:
            faces, scale = call(
                faces_kernel,
                "faces",
                out_shape=[shape(352, 128), shape(256, 128)],
                in_specs=[smem] * 5,
                out_specs=[vmem] * 2,
                scratch_shapes=[pltpu.VMEM((200, 128), f32)],
                cost_estimate=pl.CostEstimate(
                    flops=20_000_000, bytes_accessed=1_000_000, transcendentals=0
                ),
            )(slots, levels, send_counts, recv_counts, curve_counts)
        args = (
            slots, u, from_left, from_right, arrived, own, masks, faces, scale,
            index, mats, coefs,
        )
        if section < 2:
            u, left, right, own, tile = call(
                next_kernel,
                "next",
                out_shape=[shape(1024, 128), *payload],
                in_specs=[anywhere] + [vmem] * 11,
                out_specs=[vmem] * 4 + [hbm],
                scratch_shapes=[*scratch, pltpu.VMEM((128, 128), f32), sems],
            )(*args)
            kept.append(u)
    return call(
        last_kernel,
        "last",
        out_shape=shape(5, 32, 512),
        in_specs=[anywhere] + [vmem] * 13,
        out_specs=vmem,
        scratch_shapes=[*scratch, sems],
    )(*args, state, kept[0])


def solution(mesh):
    both = P(("curve", "tile"))
    rows = P(("curve", "tile"), None)
    return jax.shard_map(
        shards,
        mesh=mesh,
        in_specs=(P(None, ("curve", "tile"), None), both, rows, both, rows, rows, both, rows, rows, both),
        out_specs=P(None, ("curve", "tile"), None),
        check_vma=False,
    )
```

```python
import jax
import jax.numpy as jnp
import numpy as np
from jax import lax
from jax.experimental import pallas as pl
from jax.experimental.pallas import tpu as pltpu
from jax.sharding import PartitionSpec as P


time_step = 0.002
inner_nodes = [
    -0.8717401485096066,
    -0.5917001814331423,
    -0.20929921790247888,
    0.20929921790247888,
    0.5917001814331423,
    0.8717401485096066,
]
f32, bf16, i32 = jnp.float32, jnp.bfloat16, jnp.int32

PERM, INV, PICK, SPREAD, INDEX_ROWS = 0, 128, 256, 288, 416
CHILD, SEND_Z, RECV_Z, RECV_LIVE, CURVE_LIVE = 0, 8, 16, 24, 32


def legendre_seven(abscissa):
    before = abscissa * 0.0 + 1.0
    current = abscissa + 0.0
    for order in range(1, 7):
        before, current = (
            current,
            ((2 * order + 1) * abscissa * current - order * before) / (order + 1),
        )
    return current


def split_np(array):
    array = np.asarray(array, np.float32).astype(np.float64)
    high = array.astype(bf16).astype(np.float64)
    low = (array - high).astype(bf16).astype(np.float64)
    return high, low


def tables():
    degree = 7
    points = np.array([-1.0] + inner_nodes + [1.0])
    values = legendre_seven(points)
    weights = 2.0 / (degree * (degree + 1) * values**2)
    deriv = np.zeros((8, 8))
    for i in range(8):
        for m in range(8):
            if i != m:
                deriv[i, m] = values[i] / (values[m] * (points[i] - points[m]))
    deriv[0, 0] = -degree * (degree + 1) / 4.0
    deriv[7, 7] = degree * (degree + 1) / 4.0
    weak = -deriv
    weak[0, 0] -= 28.0
    weak[7, 7] += 28.0
    halves, projections = [], []
    for side in range(2):
        targets = (points + 2.0 * side - 1.0) / 2.0
        interp = np.ones((8, 8))
        for m in range(8):
            for other in range(8):
                if other != m:
                    interp[:, m] *= (targets - points[other]) / (points[m] - points[other])
        halves.append(interp)
        projections.append(0.5 * (interp.T * weights[None, :]) / weights[:, None])

    def child_weights(parts):
        columns = [
            np.kron(np.eye(2), np.kron(parts[a], parts[b]).T) for a in range(2) for b in range(2)
        ]
        high, low = split_np(np.concatenate(columns, axis=1))
        return np.concatenate([high, high, low], axis=0)

    def tile_weights(matrix):
        high, low = split_np(matrix.T)
        return np.block([[high, low], [high, np.zeros_like(high)]])

    along_y = np.kron(np.eye(2), np.kron(weak, np.eye(8)))
    along_z = np.kron(np.eye(16), weak)
    derivs = np.concatenate([tile_weights(along_y), tile_weights(along_z)], axis=1)
    mats = np.concatenate([child_weights(halves), child_weights(projections), derivs], axis=0)
    coefs = np.zeros((32, 128))
    for a in range(4):
        for b in range(4):
            coefs[a * 4 + b, :64] = weak[2 * a, 2 * b]
            coefs[a * 4 + b, 64:] = weak[2 * a + 1, 2 * b + 1]
            coefs[16 + a * 4 + b, :64] = weak[2 * a, 2 * b + 1]
            coefs[16 + a * 4 + b, 64:] = weak[2 * a + 1, 2 * b]

    perm = np.zeros((8, 64), np.int64)
    for code in range(8):
        for s in range(8):
            for t in range(8):
                a, c = (t, s) if code & 4 else (s, t)
                a = 7 - a if code & 1 else a
                c = 7 - c if code & 2 else c
                perm[code, 8 * s + t] = 8 * a + c
    inverse = np.argsort(perm, axis=1)
    lane = np.arange(128)
    rows = []
    for table in (perm, inverse):
        for half in range(2):
            for code in range(8):
                rows.append(table[code][lane % 64] + 64 * half)
    slot_lane = lane % 64
    i, rest = slot_lane // 8, slot_lane % 8
    for end in (7, 0):
        rows.append(64 * (i % 2) + 8 * end + rest)
        rows.append(64 * (i % 2) + 8 * rest + end)
    for kind in range(2):
        for half in range(2):
            for tile in range(4):
                first = 2 * tile + lane // 64
                second = lane % 8 if kind == 0 else (lane // 8) % 8
                rows.append(8 * first + second + 64 * half)
    index = np.repeat(np.stack(rows), 8, axis=0)
    return (
        jnp.asarray(index, i32),
        jnp.asarray(mats, f32).astype(bf16),
        jnp.asarray(coefs, f32),
    )


def take(values, index):
    return jnp.take_along_axis(values, index, axis=1, mode="promise_in_bounds")


def lanes():
    return lax.broadcasted_iota(i32, (8, 128), 1)


def split(values):
    high = values.astype(bf16)
    return high, (values - high.astype(f32)).astype(bf16)


def row(ref, start):
    return ref[pl.ds(pl.multiple_of(start, 8), 8), :]


def child_map(pieces, mats_ref, start, codes):
    high, low = split(jnp.concatenate(pieces, axis=0))
    mapped = jnp.dot(
        jnp.concatenate([high, low, high], axis=1),
        mats_ref[start : start + 384, :],
        preferred_element_type=f32,
    )
    out = []
    for f, piece in enumerate(pieces):
        total = jnp.where(codes == 4, piece, 0.0)
        for c in range(4):
            total = jnp.where(codes == c, mapped[8 * f : 8 * f + 8, 128 * c : 128 * c + 128], total)
        out.append(total)
    return out


def neighbour_part(q, sign, is_z, scale):
    normal = jnp.where(is_z, q[3], q[2]) * sign
    push = q[4] * sign
    return [
        (normal - q[0]) * scale,
        q[1] * -scale,
        (jnp.where(is_z, 0.0, push) - q[2]) * scale,
        (jnp.where(is_z, push, 0.0) - q[3]) * scale,
        (normal - q[4]) * scale,
    ]


def pack_curve(u_ref, slots, masks_ref, index_ref, tmp, left_ref, right_ref):
    low = lanes() < 64
    for side, out_ref, sign in ((0, left_ref, 1.0), (1, right_ref, -1.0)):
        for k in range(8):
            picked = []
            for s in (16 * side + k, 16 * side + k + 8):
                trace = row(u_ref, slots[s] + 768 * side)
                picked.append(take(trace, row(index_ref, slots[64 + s] + INV + 64 * side)))
            tmp[64 * side + 8 * k : 64 * side + 8 * k + 8, :] = jnp.where(low, *picked)
        q = [tmp[pl.ds(64 * side + f, 8, stride=8), :] for f in range(5)]
        scale = masks_ref[CURVE_LIVE + 8 * side : CURVE_LIVE + 8 * side + 8, :] * 14.0
        parts = [
            (sign * q[1] - q[0]) * scale,
            (sign * q[4] - q[1]) * scale,
            q[2] * -scale,
            q[3] * -scale,
            (sign * q[1] - q[4]) * scale,
        ]
        for f in range(5):
            out_ref[8 * f : 8 * f + 8, :] = parts[f]


def pack_tile(u_ref, slots, masks_ref, index_ref, mats_ref, tmp, own_ref, tile_ref, ready=None):
    low = lanes() < 64
    quarter = (lanes() % 64) // 16
    for side in range(2):
        for p in range(8):
            picked = []
            for k in range(2):
                s = 32 + 16 * side + 2 * p + k
                index = row(index_ref, slots[128 + s] * 8 + PICK + 16 * side)
                trace = take(row(u_ref, slots[s]), index)
                for a in range(1, 4):
                    other = take(row(u_ref, slots[s] + 256 * a), index)
                    trace = jnp.where(quarter == a, other, trace)
                picked.append(trace)
            pair = jnp.where(low, *picked)
            if side == 1:
                s = 48 + 2 * p
                pair = jnp.where(
                    low,
                    take(pair, row(index_ref, slots[64 + s] + INV)),
                    take(pair, row(index_ref, slots[65 + s] + INV + 64)),
                )
            tmp[64 * side + 8 * p : 64 * side + 8 * p + 8, :] = pair
    q = [tmp[pl.ds(f, 8, stride=8), :] for f in range(5)]
    if ready is not None:
        ready.wait()
    q = child_map(q, mats_ref, 0, masks_ref[CHILD : CHILD + 8, :])
    is_z = masks_ref[SEND_Z : SEND_Z + 8, :] > 0.0
    for f, part in enumerate(neighbour_part(q, -1.0, is_z, 14.0)):
        tile_ref[pl.ds(f, 8, stride=16), :] = part
        own_ref[pl.ds(f, 8, stride=8), :] = part
    q = [tmp[pl.ds(64 + f, 8, stride=8), :] for f in range(5)]
    is_z = masks_ref[RECV_Z : RECV_Z + 8, :] > 0.0
    scale = masks_ref[RECV_LIVE : RECV_LIVE + 8, :] * 14.0
    for f, part in enumerate(neighbour_part(q, 1.0, is_z, scale)):
        tile_ref[pl.ds(8 + f, 8, stride=16), :] = part


def spread(w_refs, pair, slots, s, half, end, index_ref):
    kind = slots[128 + s]
    lane = lanes()
    position = jnp.where(kind == 0, (lane // 8) % 8, lane % 8)
    at_face = position == end
    for a in range(4):
        moved = take(pair, row(index_ref, kind * 64 + SPREAD + 32 * half + 8 * a))
        block = pl.ds(pl.multiple_of(slots[s], 8), 8)
        w_refs[a][block, :] = w_refs[a][block, :] - jnp.where(at_face, moved, 0.0)


def unpack(w_refs, slots, masks_ref, index_ref, mats_ref, tmp, from_left, from_right, tile_ref, own_ref, ready):
    low = lanes() < 64
    q = [
        tile_ref[pl.ds(8 + f, 8, stride=16), :] - own_ref[pl.ds(f, 8, stride=8), :]
        for f in range(5)
    ]
    q = child_map(q, mats_ref, 384, masks_ref[CHILD : CHILD + 8, :])
    for f in range(5):
        tmp[pl.ds(f, 8, stride=8), :] = q[f]
    for side, in_ref in ((0, from_left), (1, from_right)):
        for f in range(5):
            tmp[pl.ds(64 + 64 * side + f, 8, stride=8), :] = in_ref[8 * f : 8 * f + 8, :]
    ready.wait()
    for side in range(2):
        for k in range(8):
            pair = tmp[64 + 64 * side + 8 * k : 72 + 64 * side + 8 * k, :]
            turned = pltpu.roll(pair, 64, 1)
            for s, value in ((k, (pair, turned)[side]), (k + 8, (turned, pair)[side])):
                w_ref = w_refs[3 * side]
                block = pl.ds(pl.multiple_of(slots[16 * side + s], 8), 8)
                kept = jnp.where(low, value, 0.0) if side == 0 else jnp.where(low, 0.0, value)
                w_ref[block, :] = w_ref[block, :] - kept
    for p in range(8):
        s = 48 + 2 * p
        pair = tile_ref[16 * p : 16 * p + 8, :]
        pair = jnp.where(
            low,
            take(pair, row(index_ref, slots[64 + s] + PERM)),
            take(pair, row(index_ref, slots[65 + s] + PERM + 64)),
        )
        for k in range(2):
            spread(w_refs, pair, slots, s + k, k, 0, index_ref)
    for p in range(8):
        pair = tmp[8 * p : 8 * p + 8, :]
        for k in range(2):
            spread(w_refs, pair, slots, 32 + 2 * p + k, k, 7, index_ref)


def inside(u_ref, faces_ref, mats_ref, coefs_ref, w_refs):
    fields = [[u_ref[pl.ds(256 * a + f, 32, stride=8), :] for a in range(4)] for f in range(5)]
    dens, vx, vy, vz, pres = fields

    def along(vel, start):
        stacked = [values[a] for values in (vel, pres) for a in range(4)]
        high, low = split(jnp.concatenate(stacked, axis=0))
        both = jnp.dot(
            jnp.concatenate([high, low], axis=1),
            mats_ref[768:1024, start : start + 256],
            preferred_element_type=f32,
        )
        both = both[:, :128] + both[:, 128:]
        return [both[32 * n : 32 * n + 32] for n in range(8)]

    grad_y = along(vy, 0)
    grad_z = along(vz, 256)
    grad_x = []
    for values in (vx, pres):
        plain = values
        turned = [pltpu.roll(t, 64, 1) for t in plain]
        for a in range(4):
            total = None
            for b in range(4):
                n = 4 * a + b
                term = plain[b] * coefs_ref[n : n + 1, :] + turned[b] * coefs_ref[16 + n : 17 + n, :]
                total = term if total is None else total + term
            grad_x.append(total)
    face = [faces_ref[32 * n : 32 * n + 32, :] for n in range(11)]
    ay, az, ayz, ax0, ux0, ax3, ux3, uy0, uy7, uz0, uz7 = face
    for a in range(4):
        d, x, y, z, p = (values[a] for values in fields)
        asum = ayz
        inward = -(ay * y + az * z)
        if a == 0:
            asum = asum + ax0
            inward = inward - ax0 * x
        elif a == 3:
            asum = asum + ax3
            inward = inward + ax3 * x
        diverge = grad_x[a] + grad_y[a] + grad_z[a] - inward
        out = [diverge - asum * d, grad_x[4 + a] - ayz * x, None, None, diverge - asum * p]
        if a == 0:
            out[1] = out[1] + ux0 * (p - x)
        elif a == 3:
            out[1] = out[1] - ux3 * (p + x)
        out[2] = grad_y[4 + a] + uy0 * (p - y) - uy7 * (p + y) - (asum - ay) * y
        out[3] = grad_z[4 + a] + uz0 * (p - z) - uz7 * (p + z) - (asum - az) * z
        for f in range(5):
            w_refs[a][pl.ds(f, 32, stride=8), :] = out[f]


def first_kernel(
    state_hbm, send_faces_hbm, send_counts_hbm, recv_faces_hbm, recv_orients_hbm,
    recv_counts_hbm, curve_faces_hbm, curve_orients_hbm, curve_counts_hbm, index_hbm, mats_hbm, coefs_hbm,
    u_ref, left_ref, right_ref, own_ref, tile_hbm, slots_any, masks_ref, index_ref, mats_ref, coefs_ref,
    send_faces, send_counts, recv_faces, recv_orients, recv_counts, curve_faces,
    curve_orients, curve_counts, slots, state_ref, tmp, tile_ref, sems,
):
    numbers = [
        pltpu.make_async_copy(source, target, sems.at[n])
        for n, (source, target) in enumerate(
            (
                (curve_faces_hbm, curve_faces),
                (curve_orients_hbm, curve_orients),
                (curve_counts_hbm, curve_counts),
                (send_faces_hbm, send_faces),
                (send_counts_hbm, send_counts),
                (recv_faces_hbm, recv_faces),
                (recv_orients_hbm, recv_orients),
                (recv_counts_hbm, recv_counts),
            )
        )
    ]
    arrays = [
        pltpu.make_async_copy(source, target, sems.at[8 + n])
        for n, (source, target) in enumerate(
            (
                (state_hbm, state_ref),
                (index_hbm, index_ref),
                (mats_hbm.at[pl.ds(0, 384), :], mats_ref.at[pl.ds(0, 384), :]),
                (mats_hbm.at[pl.ds(384, 640), :], mats_ref.at[pl.ds(384, 640), :]),
                (coefs_hbm, coefs_ref),
            )
        )
    ]
    for copy in numbers + arrays:
        copy.start()
    for copy in numbers:
        copy.wait()
    low = lax.broadcasted_iota(i32, (1, 128), 1) < 64

    def halves(a, b):
        return jnp.where(low, a, b)

    for side in range(2):
        live = []
        for k in range(16):
            s = 16 * side + k
            is_live = k < curve_counts[side]
            element = (curve_faces[side, k] * 10923) >> 16
            slots[s] = element * 8
            slots[64 + s] = curve_orients[side, k] * 8
            live.append(jnp.where(is_live, 1.0, 0.0))
        for k in range(8):
            at = CURVE_LIVE + 8 * side + k
            masks_ref[at : at + 1, :] = halves(live[k], live[k + 8])
    for p in range(8):
        child, kinds, recv_kinds, recv_live = [], [], [], []
        for k in range(2):
            s = 32 + 2 * p + k
            number = send_faces[k, p]
            is_live = k < send_counts[p]
            element = (number * 2185) >> 16
            rest = number - 30 * element
            is_z = rest >= 25
            slots[s] = element * 8
            slots[128 + s] = jnp.where(is_z, 1, 0)
            child.append(jnp.where(is_live, jnp.where(is_z, rest - 25, rest - 15), -1))
            kinds.append(jnp.where(is_z, 1.0, 0.0))
            s = 48 + 2 * p + k
            number = recv_faces[k, p]
            is_live = k < recv_counts[p]
            element = (number * 10923) >> 16
            is_z = number - 6 * element == 4
            slots[s] = element * 8
            slots[64 + s] = recv_orients[k, p] * 8
            slots[128 + s] = jnp.where(is_z, 1, 0)
            recv_kinds.append(jnp.where(is_z, 1.0, 0.0))
            recv_live.append(jnp.where(is_live, 1.0, 0.0))
        masks_ref[CHILD + p : CHILD + p + 1, :] = halves(*child).astype(f32)
        masks_ref[SEND_Z + p : SEND_Z + p + 1, :] = halves(*kinds)
        masks_ref[RECV_Z + p : RECV_Z + p + 1, :] = halves(*recv_kinds)
        masks_ref[RECV_LIVE + p : RECV_LIVE + p + 1, :] = halves(*recv_live)
    keep = pltpu.make_async_copy(slots, slots_any, sems.at[13])
    keep.start()
    arrays[0].wait()
    for f in range(5):
        for a in range(4):
            u_ref[pl.ds(256 * a + f, 32, stride=8), :] = state_ref[f, :, 128 * a : 128 * a + 128]
    arrays[1].wait()
    pack_tile(
        u_ref, slots, masks_ref, index_ref, mats_ref, tmp, own_ref, tile_ref, ready=arrays[2]
    )
    send = pltpu.make_async_copy(tile_ref, tile_hbm, sems.at[14])
    send.start()
    pack_curve(u_ref, slots, masks_ref, index_ref, tmp, left_ref, right_ref)
    for copy in (*arrays[3:], keep, send):
        copy.wait()


def faces_kernel(
    slots, levels, send_counts, recv_counts, curve_counts, faces_ref, scale_ref, listed
):
    listed[...] = jnp.zeros_like(listed)
    for s in range(64):
        element = slots[s] >> 3
        if s < 32:
            is_live = s % 16 < curve_counts[s // 16]
            at = 32 * (s // 16) + element
        elif s < 48:
            is_live = s % 2 < send_counts[s % 16 // 2]
            at = 96 + 64 * slots[128 + s] + element
        else:
            is_live = s % 2 < recv_counts[s % 16 // 2]
            at = 64 + 64 * slots[128 + s] + element
        listed[pl.ds(jnp.where(is_live, at, 192), 1), :] = jnp.ones((1, 128), f32)
    for e in range(32):
        scale_ref[8 * e : 8 * e + 8, :] = (
            jnp.full((8, 128), 1 << levels[e], i32).astype(f32) * time_step
        )
    lane = lax.broadcasted_iota(i32, (32, 128), 1)
    on = [listed[32 * f : 32 * f + 32, :] for f in range(6)]
    where_0 = [lane < 64, (lane // 8) % 8 == 0, lane % 8 == 0]
    where_7 = [lane >= 64, (lane // 8) % 8 == 7, lane % 8 == 7]

    def keep(test, values):
        return jnp.where(test, values, 0.0)

    ay = keep(where_0[1], 14.0 * on[2])
    az = keep(where_0[2], 14.0 * on[4])
    values = [
        ay,
        az,
        ay + az,
        keep(where_0[0], 14.0 * on[0]),
        keep(where_0[0], 28.0 - 14.0 * on[0]),
        keep(where_7[0], 14.0 * on[1]),
        keep(where_7[0], 28.0 - 14.0 * on[1]),
        keep(where_0[1], 28.0 - 14.0 * on[2]),
        keep(where_7[1], 28.0 - 28.0 * on[3]),
        keep(where_0[2], 28.0 - 14.0 * on[4]),
        keep(where_7[2], 28.0 - 28.0 * on[5]),
    ]
    for n, value in enumerate(values):
        faces_ref[32 * n : 32 * n + 32, :] = value


def next_kernel(
    slots_any, u_ref, from_left, from_right, arrived_ref, sent_ref, masks_ref, faces_ref, scale_ref,
    index_ref, mats_ref, coefs_ref,
    out_ref, left_ref, right_ref, own_ref, tile_hbm, w_0, w_1, w_2, w_3, tmp, slots, tile_ref, sems,
):
    w_refs = (w_0, w_1, w_2, w_3)
    fetch = pltpu.make_async_copy(slots_any, slots, sems.at[0])
    fetch.start()
    inside(u_ref, faces_ref, mats_ref, coefs_ref, w_refs)
    unpack(
        w_refs, slots, masks_ref, index_ref, mats_ref, tmp, from_left, from_right, arrived_ref, sent_ref,
        fetch,
    )
    for a in range(4):
        out_ref[256 * a : 256 * a + 256, :] = w_refs[a][...] * scale_ref[...]
    pack_tile(out_ref, slots, masks_ref, index_ref, mats_ref, tmp, own_ref, tile_ref)
    send = pltpu.make_async_copy(tile_ref, tile_hbm, sems.at[1])
    send.start()
    pack_curve(out_ref, slots, masks_ref, index_ref, tmp, left_ref, right_ref)
    send.wait()


def last_kernel(
    slots_any, u_ref, from_left, from_right, arrived_ref, sent_ref, masks_ref, faces_ref, scale_ref,
    index_ref, mats_ref, coefs_ref, state_ref, first_ref,
    out_ref, w_0, w_1, w_2, w_3, tmp, slots, sems,
):
    w_refs = (w_0, w_1, w_2, w_3)
    fetch = pltpu.make_async_copy(slots_any, slots, sems.at[0])
    fetch.start()
    inside(u_ref, faces_ref, mats_ref, coefs_ref, w_refs)
    unpack(
        w_refs, slots, masks_ref, index_ref, mats_ref, tmp, from_left, from_right, arrived_ref, sent_ref,
        fetch,
    )
    scale = scale_ref[pl.ds(0, 32, stride=8), :] * (1.0 / 6.0)
    for f in range(5):
        for a in range(4):
            at = (pl.ds(256 * a + f, 32, stride=8), slice(None))
            column = slice(128 * a, 128 * a + 128)
            out_ref[f, :, column] = (
                state_ref[f, :, column]
                + first_ref[at]
                + 0.5 * u_ref[at]
                + w_refs[a][pl.ds(f, 32, stride=8), :] * scale
            )


def shards(
    state, levels, send_faces, send_counts, recv_faces, recv_orients, recv_counts,
    curve_faces, curve_orients, curve_counts,
):
    index, mats, coefs = tables()
    vmem = pl.BlockSpec(memory_space=pltpu.VMEM)
    smem = pl.BlockSpec(memory_space=pltpu.SMEM)
    hbm = pl.BlockSpec(memory_space=pltpu.HBM)
    anywhere = pl.BlockSpec(memory_space=pl.ANY)

    def shape(*dims, kind=f32):
        return jax.ShapeDtypeStruct(dims, kind)

    def call(kernel, name, **kwargs):
        return pl.pallas_call(
            kernel,
            name=name,
            compiler_params=pltpu.CompilerParams(vmem_limit_bytes=16 * 1024 * 1024),
            **kwargs,
        )

    payload = [shape(40, 128)] * 2 + [shape(64, 128), shape(128, 128)]
    n_curve = lax.axis_size("curve")
    rightward = [(i, i + 1) for i in range(n_curve - 1)]
    leftward = [(i + 1, i) for i in range(n_curve - 1)]

    def exchange(left, right, tile):
        arrived = lax.all_to_all(
            tile.reshape(8, 16, 128), "tile", split_axis=0, concat_axis=0, tiled=True
        )
        from_left = lax.ppermute(right, "curve", rightward)
        from_right = lax.ppermute(left, "curve", leftward)
        return from_left, from_right, arrived.reshape(128, 128)

    numbers = [
        send_faces.T, send_counts, recv_faces.T, recv_orients.T, recv_counts,
        curve_faces, curve_orients, curve_counts,
    ]
    u, left, right, own, tile, slots, masks, index, mats, coefs = call(
        first_kernel,
        "first",
        out_shape=[shape(1024, 128), *payload, shape(256, kind=i32), shape(48, 128)]
        + [shape(*x.shape, kind=x.dtype) for x in (index, mats, coefs)],
        in_specs=[hbm] * 12,
        out_specs=[vmem] * 4 + [hbm, anywhere] + [vmem] * 4,
        scratch_shapes=[pltpu.SMEM(x.shape, i32) for x in numbers] + [pltpu.SMEM((256,), i32)]
        + [
            pltpu.VMEM(state.shape, f32),
            pltpu.VMEM((128, 128), f32),
            pltpu.VMEM((128, 128), f32),
            pltpu.SemaphoreType.DMA((15,)),
        ],
    )(*[pltpu.with_memory_space_constraint(x, pltpu.HBM) for x in (state, *numbers, index, mats, coefs)])
    scratch = [pltpu.VMEM((256, 128), f32)] * 4
    scratch += [pltpu.VMEM((192, 128), f32), pltpu.SMEM((256,), i32)]
    sems = pltpu.SemaphoreType.DMA((2,))
    kept = []
    for section in range(3):
        from_left, from_right, arrived = exchange(left, right, tile)
        if section == 0:
            faces, scale = call(
                faces_kernel,
                "faces",
                out_shape=[shape(352, 128), shape(256, 128)],
                in_specs=[smem] * 5,
                out_specs=[vmem] * 2,
                scratch_shapes=[pltpu.VMEM((200, 128), f32)],
                cost_estimate=pl.CostEstimate(
                    flops=20_000_000, bytes_accessed=1_000_000, transcendentals=0
                ),
            )(slots, levels, send_counts, recv_counts, curve_counts)
        args = (
            slots, u, from_left, from_right, arrived, own, masks, faces, scale,
            index, mats, coefs,
        )
        if section < 2:
            u, left, right, own, tile = call(
                next_kernel,
                "next",
                out_shape=[shape(1024, 128), *payload],
                in_specs=[anywhere] + [vmem] * 11,
                out_specs=[vmem] * 4 + [hbm],
                scratch_shapes=[*scratch, pltpu.VMEM((128, 128), f32), sems],
            )(*args)
            kept.append(u)
    return call(
        last_kernel,
        "last",
        out_shape=shape(5, 32, 512),
        in_specs=[anywhere] + [vmem] * 13,
        out_specs=vmem,
        scratch_shapes=[*scratch, sems],
    )(*args, state, kept[0])


def solution(mesh):
    both = P(("curve", "tile"))
    rows = P(("curve", "tile"), None)
    return jax.shard_map(
        shards,
        mesh=mesh,
        in_specs=(P(None, ("curve", "tile"), None), both, rows, both, rows, rows, both, rows, rows, both),
        out_specs=P(None, ("curve", "tile"), None),
        check_vma=False,
    )
```
